32 devices in a mesh: dp: 4 (over y, x), ctx: 4 (over z), tensor: 2 (over core).
Axes of the slice: x: 2, y: 2, z: 4, core: 2. Of those that a mesh axis runs over, the one named last changes fastest.
Arguments:
- tokens: bfloat16 [8, 2048, 1536], P('dp', 'ctx'), may hold values from -6 to 6
- cotangent: bfloat16 [8, 2048, 1536], P('dp', 'ctx'), may hold values from -6 to 6
- lengths: int32 [8], P('dp'), may hold values from 512 to 2048, as said below
- slot_adapter_index: int32 [8], P('dp'), may hold values from 0 to 7
- input_norm_gain: float32 [1536], replicated, may hold values from 0.5 to 1.5
- gate_weight_matrix: bfloat16 [1536, 3072], P('dp', 'tensor'), may hold values from -0.15625 to 0.15625
- inner_weight_matrix: bfloat16 [1536, 3072], P('dp', 'tensor'), may hold values from -0.15625 to 0.15625
- state_map_weight: bfloat16 [1536, 256], P('dp'), may hold values from -0.15625 to 0.15625
- step_size_weight: bfloat16 [1536, 48], P('dp', 'tensor'), may hold values from -0.15625 to 0.15625
- output_projection_weight: bfloat16 [1536, 3072], P('dp', 'tensor'), may hold values from -0.109375 to 0.109375
- inner_channel_taps: float32 [4, 3072], P(None, 'tensor'), may hold values from -3 to 3
- state_map_taps: float32 [4, 256], replicated, may hold values from -3 to 3
- inner_conv_bias: float32 [3072], P('tensor'), may hold values from -2 to 2
- state_map_conv_bias: float32 [256], replicated, may hold values from -2 to 2
- step_size_bias: float32 [48], P('tensor'), may hold values from -2 to 0
- log_decay_rate: float32 [48], P('tensor'), may hold values from -12 to -2
- head_skip_gain: float32 [48], P('tensor'), may hold values from 0.5 to 1.5
- gated_norm_gain: float32 [3072], P('tensor'), may hold values from 0.5 to 1.5
- adapter_in_down_maps: bfloat16 [8, 1536, 16], replicated, may hold values from -0.15625 to 0.15625
- adapter_in_up_maps: bfloat16 [8, 2, 16, 3072], P(None, None, None, 'tensor'), may hold values from -1.5 to 1.5
- adapter_out_down_maps: bfloat16 [8, 3072, 16], P(None, 'tensor'), may hold values from -0.109375 to 0.109375
- adapter_out_up_maps: bfloat16 [8, 16, 1536], replicated, may hold values from -1.5 to 1.5
Outputs:
- result: bfloat16 [8, 2048, 1536], P('dp', 'ctx')
- grad_tokens: float32 [8, 2048, 1536], P('dp', 'ctx')
- grad_lora_in_down: float32 [8, 1536, 16], replicated
- grad_lora_in_up: float32 [8, 2, 16, 3072], P(None, None, None, 'tensor')
- grad_lora_out_down: float32 [8, 3072, 16], P(None, 'tensor')
- grad_lora_out_up: float32 [8, 16, 1536], replicated
The draws below stay inside these ranges and needn't reach their ends.
Inputs may be any that keep to these rules, and one draw needn't show every extreme that they name: Each slot holds one sequence in its first lengths positions; in every draw some slot has length 2048.
All inputs are finite; a program needn't handle non-finite values.
Results may differ from the reference program's by a relative error of at most 0.006.
The reference program's roundings to bfloat16 on the way count: a program that leaves them out, or rounds other values in their place, can miss the bound.
Values may be sent and summed in bfloat16 or wider, within the bound.
A program may use at most 320 MiB of HBM per device.

```python
import math
import jax
import jax.numpy as jnp
from jax import lax

MODEL_FEATURES = 1536
MIXER_WIDTH = 3072
H = 48
P_SIZE = 64
N = 128
K = 4
GROUP = 256
ADAPTER_RANK = 16
ADAPTER_COUNT = 8
SLOTS = 8
SLOT = 2048
MINLEN = 512


def draw_lengths(key, part):
    first_key, second_key = jax.random.split(key)
    drawn_len = jax.random.randint(first_key, (SLOTS,), MINLEN, SLOT + 1)
    fullest = jax.random.randint(second_key, (), 0, SLOTS)
    return jnp.where(jnp.arange(SLOTS) == fullest, SLOT, drawn_len).astype(jnp.int32)


def draw_log_decay_rate(key, part):
    first_key, second_key = jax.random.split(key)
    slow_share = 0.5
    chooser = jax.random.uniform(first_key, (H,), dtype=jnp.float32)
    spread = jax.random.uniform(second_key, (H,), dtype=jnp.float32, minval=0.0, maxval=math.log(2.0))
    slow_level = math.log(0.25 / SLOT)
    fast_level = math.log(1.0 / 32.0)
    return (jnp.where(chooser < slow_share, slow_level, fast_level) + spread).astype(jnp.float32)


def touch_ends(drawn, rng, low, largest):
    longest = drawn.shape.index(max(drawn.shape))
    spots = []
    for shift in (0, 1):
        where = [jax.random.randint(jax.random.fold_in(rng, axis), (), 0, length) for axis, length in enumerate(drawn.shape)]
        where[longest] = (where[longest] + shift) % drawn.shape[longest]
        spots.append(tuple(where))
    return drawn.at[spots[0]].set(low).at[spots[1]].set(largest)


def steps_of(key, dims, cuts, low, largest):
    level, own = 1.0, jax.random.fold_in(key, 6)
    for axis_at, parts in cuts:
        heights = jnp.exp(jax.random.uniform(jax.random.fold_in(own, axis_at), (parts,), jnp.float32, low / len(cuts), largest / len(cuts)))
        level = level * jnp.repeat(heights, dims[axis_at] // parts).reshape([-1 if axis == axis_at else 1 for axis in range(len(dims))])
    return level


def centred(rng, extent, deviation, limit, cuts=(), held_as=jnp.bfloat16):
    values = deviation * jax.random.normal(rng, extent, jnp.float32)
    if cuts:
        values = values * steps_of(rng, extent, cuts, -0.22, 0.18)
    return jnp.clip(values, -limit, limit).astype(held_as)


def setup_inputs(seed: int = 0) -> dict:
    key_list = jax.random.split(jax.random.key(seed), 23)
    tokens = centred(key_list[0], (SLOTS, SLOT, MODEL_FEATURES), 1.0, 6.0, ((0, 4), (1, 4)))
    cotangent = centred(key_list[1], (SLOTS, SLOT, MODEL_FEATURES), 1.0, 6.0, ((0, 4), (1, 4)))
    lengths = draw_lengths(jax.random.fold_in(key_list[22], 71), 0)
    slot_adapter_index = touch_ends(jax.random.randint(key_list[3], (SLOTS,), 0, ADAPTER_COUNT), jax.random.fold_in(key_list[3], 1), 0, ADAPTER_COUNT - 1).astype(jnp.int32)
    input_norm_gain = jnp.clip(1.0 + 0.1 * jax.random.normal(key_list[4], (MODEL_FEATURES,), jnp.float32), 0.5, 1.5)
    gate_weight_matrix = centred(key_list[5], (MODEL_FEATURES, MIXER_WIDTH), MODEL_FEATURES ** -0.5, 0.15625, ((0, 4), (1, 2)))
    inner_weight_matrix = centred(key_list[6], (MODEL_FEATURES, MIXER_WIDTH), MODEL_FEATURES ** -0.5, 0.15625, ((0, 4), (1, 2)))
    state_map_weight = centred(key_list[7], (MODEL_FEATURES, 2 * N), MODEL_FEATURES ** -0.5, 0.15625, ((0, 4),))
    step_size_weight = centred(key_list[8], (MODEL_FEATURES, H), MODEL_FEATURES ** -0.5, 0.15625, ((0, 4), (1, 2)))
    output_projection_weight = centred(key_list[9], (MODEL_FEATURES, MIXER_WIDTH), MIXER_WIDTH ** -0.5, 0.109375, ((0, 4), (1, 2)))
    inner_channel_taps = centred(key_list[10], (K, MIXER_WIDTH), 0.5, 3.0, ((1, 2),), jnp.float32)
    state_map_taps = centred(key_list[11], (K, 2 * N), 0.5, 3.0, (), jnp.float32)
    inner_conv_bias = centred(key_list[12], (MIXER_WIDTH,), 0.3, 2.0, ((0, 2),), jnp.float32)
    state_map_conv_bias = centred(key_list[13], (2 * N,), 0.3, 2.0, (), jnp.float32)
    step_size_bias = jnp.clip(-2.0 + 2.0 * jax.random.uniform(key_list[14], (H,), jnp.float32) ** steps_of(key_list[14], (H,), ((0, 2),), -0.2, 0.2), -2.0, 0.0)
    log_decay_rate = draw_log_decay_rate(jax.random.fold_in(key_list[22], 71), 0)
    head_skip_gain = jnp.clip(0.5 + 1.0 * jax.random.uniform(key_list[16], (H,), jnp.float32) ** steps_of(key_list[16], (H,), ((0, 2),), -0.2, 0.2), 0.5, 1.5)
    gated_norm_gain = jnp.clip(1.0 + 0.1 * jax.random.normal(key_list[17], (MIXER_WIDTH,), jnp.float32), 0.5, 1.5)
    adapter_in_down_maps = centred(key_list[18], (ADAPTER_COUNT, MODEL_FEATURES, ADAPTER_RANK), MODEL_FEATURES ** -0.5, 0.15625)
    adapter_in_up_maps = centred(key_list[19], (ADAPTER_COUNT, 2, ADAPTER_RANK, MIXER_WIDTH), ADAPTER_RANK ** -0.5, 1.5, ((3, 2),))
    adapter_out_down_maps = centred(key_list[20], (ADAPTER_COUNT, MIXER_WIDTH, ADAPTER_RANK), MIXER_WIDTH ** -0.5, 0.109375, ((1, 2),))
    adapter_out_up_maps = centred(key_list[21], (ADAPTER_COUNT, ADAPTER_RANK, MODEL_FEATURES), ADAPTER_RANK ** -0.5, 1.5)
    return {"tokens": tokens, "cotangent": cotangent, "lengths": lengths, "slot_adapter_index": slot_adapter_index, "input_norm_gain": input_norm_gain, "gate_weight_matrix": gate_weight_matrix, "inner_weight_matrix": inner_weight_matrix, "state_map_weight": state_map_weight, "step_size_weight": step_size_weight, "output_projection_weight": output_projection_weight, "inner_channel_taps": inner_channel_taps, "state_map_taps": state_map_taps, "inner_conv_bias": inner_conv_bias, "state_map_conv_bias": state_map_conv_bias, "step_size_bias": step_size_bias, "log_decay_rate": log_decay_rate, "head_skip_gain": head_skip_gain, "gated_norm_gain": gated_norm_gain, "adapter_in_down_maps": adapter_in_down_maps, "adapter_in_up_maps": adapter_in_up_maps, "adapter_out_down_maps": adapter_out_down_maps, "adapter_out_up_maps": adapter_out_up_maps}


@jax.custom_vjp
def low(v):
    return lax.optimization_barrier(v.astype(jnp.bfloat16)).astype(jnp.float32)

@jax.custom_vjp
def low_back(v):
    return v

def low_keep(v):
    return (low(v), None)

def low_pass(kept, grad):
    return (grad,)

def back_keep(v):
    return (v, None)

def back_low(kept, grad):
    return (low(grad),)
low.defvjp(low_keep, low_pass)
low_back.defvjp(back_keep, back_low)
EPSILON = 1e-05
HIGHEST_PRECISION = lax.Precision.HIGHEST

def matmul_high(left, right):
    return jnp.dot(left, right, precision=HIGHEST_PRECISION)

def scan_mixer(x_conv, b_matrix, c_matrix, step_val, decay_rate, head_skip_gain):
    total_len = x_conv.shape[0]
    block_count = total_len // GROUP
    pieces = (x_conv.reshape(block_count, GROUP, H, P_SIZE), b_matrix.reshape(block_count, GROUP, N), c_matrix.reshape(block_count, GROUP, N), step_val.reshape(block_count, GROUP, H))
    position = jnp.arange(GROUP)
    causal = (position[:, None] >= position[None, :])[:, :, None]

    def block_step(carry_state, piece_set):
        x_part, b_part, c_part, step_part = piece_set
        cumulative = jnp.cumsum(step_part * decay_rate[None, :], axis=0)
        scores = matmul_high(c_part, b_part.T)
        spread_log = jnp.where(causal, cumulative[:, None, :] - cumulative[None, :, :], 0.0)
        decay_table = jnp.where(causal, jnp.exp(spread_log), 0.0)
        mixing = low(scores[:, :, None] * decay_table * step_part[None, :, :])
        inside = jnp.einsum('tsh,shp->thp', mixing, x_part, precision=HIGHEST_PRECISION)
        carried = jnp.einsum('tn,hpn->thp', c_part, carry_state, precision=HIGHEST_PRECISION) * jnp.exp(cumulative)[:, :, None]
        tail_weight = jnp.exp(cumulative[-1][None, :] - cumulative) * step_part
        fresh_state = jnp.einsum('sh,shp,sn->hpn', tail_weight, x_part, b_part, precision=HIGHEST_PRECISION)
        next_state = jnp.exp(cumulative[-1])[:, None, None] * carry_state + fresh_state
        return (next_state, inside + carried + head_skip_gain[None, :, None] * x_part)
    initial = jnp.zeros((H, P_SIZE, N), jnp.float32)
    _, outputs = lax.scan(jax.checkpoint(block_step), initial, pieces)
    return outputs.reshape(total_len, H * P_SIZE)

def reference(tokens, cotangent, lengths, slot_adapter_index, input_norm_gain, gate_weight_matrix, inner_weight_matrix, state_map_weight, step_size_weight, output_projection_weight, inner_channel_taps, state_map_taps, inner_conv_bias, state_map_conv_bias, step_size_bias, log_decay_rate, head_skip_gain, gated_norm_gain, adapter_in_down_maps, adapter_in_up_maps, adapter_out_down_maps, adapter_out_up_maps):
    gate_float = gate_weight_matrix.astype(jnp.float32)
    inner_float = inner_weight_matrix.astype(jnp.float32)
    bc_float = state_map_weight.astype(jnp.float32)
    step_float = step_size_weight.astype(jnp.float32)
    out_float = output_projection_weight.astype(jnp.float32)
    conv_weight = jnp.concatenate([inner_channel_taps, state_map_taps], axis=1)
    conv_bias = jnp.concatenate([inner_conv_bias, state_map_conv_bias])
    decay_rate = -jnp.exp(log_decay_rate)
    adapter_tables = (adapter_in_down_maps.astype(jnp.float32), adapter_in_up_maps.astype(jnp.float32), adapter_out_down_maps.astype(jnp.float32), adapter_out_up_maps.astype(jnp.float32))

    def forward(slot_tokens, in_down, in_up, out_down, out_up, live_mask):
        in_scale = lax.rsqrt(lax.optimization_barrier(jnp.mean(slot_tokens * slot_tokens, axis=-1, keepdims=True)) + EPSILON)
        normed = low(slot_tokens * in_scale * input_norm_gain[None, :])
        low_in = low(matmul_high(normed, in_down))
        gate_val = low_back(matmul_high(normed, gate_float) + matmul_high(low_in, in_up[0]))
        inner_val = low_back(matmul_high(normed, inner_float) + matmul_high(low_in, in_up[1]))
        bc_val = matmul_high(normed, bc_float)
        step_raw = low_back(matmul_high(normed, step_float))
        conv_input = low(jnp.concatenate([inner_val, bc_val], axis=1))
        padded = jnp.pad(conv_input, ((K - 1, 0), (0, 0)))
        conv_val = jnp.zeros_like(conv_input) + conv_bias[None, :]
        for offset in range(K):
            conv_val = conv_val + conv_weight[offset][None, :] * padded[offset:offset + SLOT]
        activated = jax.nn.silu(conv_val)
        x_conv = low(activated[:, :MIXER_WIDTH]).reshape(SLOT, H, P_SIZE)
        b_matrix = low(activated[:, MIXER_WIDTH:MIXER_WIDTH + N])
        c_matrix = low(activated[:, MIXER_WIDTH + N:])
        step_val = jax.nn.softplus(step_raw + step_size_bias[None, :])
        mixer_out = low_back(scan_mixer(x_conv, b_matrix, c_matrix, step_val, decay_rate, head_skip_gain))
        gated_val = mixer_out * jax.nn.silu(gate_val)
        gate_scale = lax.rsqrt(lax.optimization_barrier(jnp.mean(gated_val * gated_val, axis=-1, keepdims=True)) + EPSILON)
        normed_out = low(gated_val * gate_scale * gated_norm_gain[None, :])
        low_out = low(matmul_high(normed_out, out_down))
        branch = matmul_high(normed_out, out_float.T) + matmul_high(low_out, out_up)
        return slot_tokens + live_mask[:, None] * branch

    def per_slot(totals, slot_data):
        slot_tokens, slot_cotangent, slot_length, adapter = slot_data
        live_mask = (jnp.arange(SLOT) < slot_length).astype(jnp.float32)
        chosen = tuple((table[adapter] for table in adapter_tables))

        def closed(slot_input, in_down, in_up, out_down, out_up):
            return forward(slot_input, in_down, in_up, out_down, out_up, live_mask)
        output, pull_back = jax.vjp(closed, slot_tokens.astype(jnp.float32), chosen[0], chosen[1], chosen[2], chosen[3])
        grads = pull_back(slot_cotangent.astype(jnp.float32))
        totals = tuple((running_sum.at[adapter].add(piece_grad) for running_sum, piece_grad in zip(totals, grads[1:])))
        return (totals, (output.astype(jnp.bfloat16), grads[0]))
    zero_sums = tuple((jnp.zeros_like(table) for table in adapter_tables))
    totals, (outputs, grad_tokens) = lax.scan(per_slot, zero_sums, (tokens, cotangent, lengths, slot_adapter_index))
    return (outputs, grad_tokens, totals[0], totals[1], totals[2], totals[3])
```

```python
import functools

import jax
import jax.numpy as jnp
from jax import lax
from jax.experimental import pallas as pl
from jax.experimental.pallas import tpu as pltpu
from jax.sharding import PartitionSpec as P

MIXER_WIDTH = 3072
GROUP = 256
EPSILON = 1e-05
LANES = 128
HALO = 8
TURN = 8
F32 = jnp.float32
BF16 = jnp.bfloat16
VMEM_LIMIT = 60 * 1024 * 1024


def shifted(block, axis, distance):
    devices = range(lax.axis_size(axis))
    route = [(i - distance, i) for i in devices if i - distance in devices]
    return lax.ppermute(block, axis, route)


def partner(value, axis):
    size = lax.axis_size(axis)
    return lax.ppermute(value, axis, [(i, (i + 1) % size) for i in range(size)])


def swapped(value, axis, distance):
    return lax.ppermute(value, axis, [(i, i ^ distance) for i in range(lax.axis_size(axis))])


def rows_of_all(block):
    half = block.shape[0] // 2
    first, second = swapped(block, "dp", 1), swapped(block, "dp", 2)
    return block, first, second, swapped(first[:half], "dp", 2), swapped(second[half:], "dp", 1)


def dot(a, b):
    return jnp.dot(a, b, preferred_element_type=F32)


def dot_nt(a, b):
    return lax.dot_general(a, b, (((1,), (1,)), ((), ())), preferred_element_type=F32)


def dot_tn(a, b):
    return lax.dot_general(a, b, (((0,), (0,)), ((), ())), preferred_element_type=F32)


def split(value):
    high = value.astype(BF16)
    return high, (value - high.astype(F32)).astype(BF16)


def exact_dot(value, table):
    high, low = split(value)
    return dot(high, table) + dot(low, table)


def sigmoid(value):
    return 1.0 / (1.0 + jnp.exp(-value))


def silu_grad(value):
    g = sigmoid(value)
    return g * (1.0 + value * (1.0 - g))


def params(**more):
    return pltpu.CompilerParams(vmem_limit_bytes=VMEM_LIMIT, **more)


ANYWHERE = pl.BlockSpec(memory_space=pl.ANY)


def assemble(place, parts, table, sem):
    rows = parts[0].shape[0]
    half = rows // 2
    copies = []
    for step, first, part in zip((0, 1, 2, 3, 3), (0, 0, 0, 0, half), parts):
        at = pl.multiple_of((place ^ step) * rows + first, half)
        copies.append(pltpu.make_async_copy(part, table.at[pl.ds(at, part.shape[0])], sem))
    for copy in copies:
        copy.start()
    for copy in copies:
        copy.wait()


def whole(shape):
    return pl.BlockSpec(shape, lambda *_: (0,) * len(shape))


def running_sum(value, backwards=False):
    rows = value.shape[0]
    i = lax.broadcasted_iota(jnp.int32, (rows, rows), 0)
    j = lax.broadcasted_iota(jnp.int32, (rows, rows), 1)
    table = jnp.where(i <= j if backwards else i >= j, 1.0, 0.0).astype(F32)
    return jnp.dot(table, value, precision=lax.Precision.HIGHEST, preferred_element_type=F32)


def conv_taps(ext_ref, taps_ref, bias_ref, lanes, tap_count):
    value = jnp.zeros((GROUP, LANES), F32) + bias_ref[:, lanes]
    for k in range(tap_count):
        start = HALO - (tap_count - 1) + k
        value = value + taps_ref[k : k + 1, lanes] * ext_ref[start : start + GROUP, lanes]
    return value


def enter_kernel(
    tap_count, index_ref, tok_ref, halo_ref, gain_ref, w0, w1, w2, w3, w4, down_ref, up_ref, taps_ref,
    bias_ref, step_bias_ref, rate_ref, e_ref,
    normed_ref, low_ref, conv_ref, x_ref, bc_ref, raw_ref, cum_ref, loc_ref, before_ref, full_ref,
    ext, state, w_ref, sem, out_sem,
):
    b = pl.program_id(1)
    keep = pltpu.make_async_copy(w_ref, full_ref, out_sem)

    @pl.when((pl.program_id(0) == 0) & (b == 0))
    def _():
        assemble(index_ref[pl.num_programs(0)], (w0, w1, w2, w3, w4), w_ref, sem)
        keep.start()

    width = x_ref.shape[-1]
    conv_width = conv_ref.shape[-1]

    def project(tok):
        tok = tok.astype(F32)
        scale = lax.rsqrt(jnp.mean(tok * tok, axis=-1, keepdims=True) + EPSILON)
        normed = (tok * scale * gain_ref[...]).astype(BF16)
        low = dot(normed, down_ref[0]).astype(BF16)
        inner = dot(normed, w_ref[:, :width]) + dot(low, up_ref[0, 1])
        rest = dot(normed, w_ref[:, width:])
        return normed, low, inner, rest

    @pl.when(b == 0)
    def _():
        _, _, inner, rest = project(halo_ref[0])
        ext[:HALO, :width] = inner.astype(BF16).astype(F32)
        ext[:HALO, width:] = rest[:, : conv_width - width].astype(BF16).astype(F32)
        state[...] = jnp.zeros_like(state)

    @pl.when(b > 0)
    def _():
        ext[:HALO] = ext[GROUP:]

    before_ref[0, 0] = ext[:HALO].astype(BF16)
    normed, low, inner, rest = project(tok_ref[0])
    normed_ref[0] = normed
    low_ref[0] = low
    inner = inner.astype(BF16)
    states = rest[:, : conv_width - width].astype(BF16)
    conv_ref[0, :, :width] = inner
    conv_ref[0, :, width:] = states
    ext[HALO:, :width] = inner.astype(F32)
    ext[HALO:, width:] = states.astype(F32)
    raw = rest[:, conv_width - width :]
    raw_ref[0] = raw
    step = jax.nn.softplus(raw + step_bias_ref[...])
    cum = running_sum(step * rate_ref[...])
    cum_ref[0] = cum
    last = cum[GROUP - 1 :]
    tail = jnp.exp(last - cum) * step

    for at in range(width, conv_width, LANES):
        lanes = slice(at, at + LANES)
        value = conv_taps(ext, taps_ref, bias_ref, lanes, tap_count)
        bc_ref[0, :, at - width : at - width + LANES] = (value * sigmoid(value)).astype(BF16)
    b_mat = bc_ref[0, :, : bc_ref.shape[-1] // 2]
    tail_high, tail_low = split(tail)
    decay_high, decay_low = split(jnp.broadcast_to(jnp.exp(last), (HALO, LANES)))
    for at in range(0, width, LANES):
        lanes = slice(at, at + LANES)
        value = conv_taps(ext, taps_ref, bias_ref, lanes, tap_count)
        x = (value * sigmoid(value)).astype(BF16)
        x_ref[0, :, lanes] = x
        table = e_ref[:, lanes]
        weighted = (x.astype(F32) * (dot(tail_high, table) + dot(tail_low, table))).astype(BF16)
        decay = (dot(decay_high, table) + dot(decay_low, table))[:1]
        new = decay * state[:, lanes] + dot_tn(b_mat, weighted)
        state[:, lanes] = new
        loc_ref[0, 0, :, lanes] = new

    @pl.when((pl.program_id(0) == pl.num_programs(0) - 1) & (b == pl.num_programs(1) - 1))
    def _():
        keep.wait()


def enter(index, tokens, halo, gain, w, down, up, taps, bias, step_bias, rate, e, width, conv_width):
    s, length, model = tokens.shape
    blocks = length // GROUP
    rank = down.shape[-1]
    states = (conv_width - width) // 2
    rows = lambda n: pl.BlockSpec((1, GROUP, n), lambda i, j, _: (i, j, 0))
    out = lambda n, kind: jax.ShapeDtypeStruct((s, length, n), kind)
    return pl.pallas_call(
        functools.partial(enter_kernel, 4),
        grid_spec=pltpu.PrefetchScalarGridSpec(
            num_scalar_prefetch=1,
            grid=(s, blocks),
            in_specs=[
                rows(model),
                pl.BlockSpec((1, HALO, model), lambda i, j, _: (i, 0, 0)),
                whole(gain.shape),
                *[ANYWHERE] * 5,
                pl.BlockSpec((1, model, rank), lambda i, j, idx: (idx[i], 0, 0)),
                pl.BlockSpec((1, 2, rank, width), lambda i, j, idx: (idx[i], 0, 0, 0)),
                whole(taps.shape),
                whole(bias.shape),
                whole(step_bias.shape),
                whole(rate.shape),
                whole(e.shape),
            ],
            out_specs=[
                rows(model), rows(rank), rows(conv_width), rows(width), rows(2 * states),
                rows(LANES), rows(LANES),
                pl.BlockSpec((1, 1, states, width), lambda i, j, _: (i, j, 0, 0)),
                pl.BlockSpec((1, 1, HALO, conv_width), lambda i, j, _: (i, j, 0, 0)),
                ANYWHERE,
            ],
            scratch_shapes=[
                pltpu.VMEM((GROUP + HALO, conv_width), F32),
                pltpu.VMEM((states, width), F32),
                pltpu.VMEM((model, w[0].shape[1]), BF16),
                pltpu.SemaphoreType.DMA,
                pltpu.SemaphoreType.DMA,
            ],
        ),
        out_shape=[
            out(model, BF16), out(rank, BF16), out(conv_width, BF16), out(width, BF16),
            out(2 * states, BF16), out(LANES, F32), out(LANES, F32),
            jax.ShapeDtypeStruct((s, blocks, states, width), F32),
            jax.ShapeDtypeStruct((s, blocks, HALO, conv_width), BF16),
            jax.ShapeDtypeStruct((model, w[0].shape[1]), BF16),
        ],
        compiler_params=params(),
        name="enter",
        cost_estimate=pl.CostEstimate(flops=15_000_000_000, bytes_accessed=30_000_000, transcendentals=0),
    )(index, tokens, halo, gain, *w, down, up, taps, bias, step_bias, rate, e)


def inside_kernel(x_ref, bc_ref, raw_ref, cum_ref, step_bias_ref, skip_ref, y_ref, cum_t, step_t, scores):
    states = bc_ref.shape[-1] // 2
    heads_at = x_ref.shape[-1] // 64
    cum = cum_ref[0]
    step = jax.nn.softplus(raw_ref[0] + step_bias_ref[...])
    cum_t[...] = cum.T
    step_t[...] = step.T
    scores[...] = dot_nt(bc_ref[0, :, states:], bc_ref[0, :, :states])
    lane = lax.broadcasted_iota(jnp.int32, (GROUP, LANES), 1)
    causal = lax.broadcasted_iota(jnp.int32, (LANES, LANES), 0) >= lax.broadcasted_iota(
        jnp.int32, (LANES, LANES), 1
    )
    half = GROUP // 2

    @pl.loop(0, heads_at // TURN)
    def _(turn):
        rolled = pltpu.roll(cum, (LANES - TURN * turn) % LANES, 1)
        rows = pl.ds(pl.multiple_of(turn * TURN, TURN), TURN)
        cum_rows = cum_t[rows, :]
        step_rows = step_t[rows, :]
        for pair in range(TURN // 2):
            lanes = pl.ds(pl.multiple_of(turn * (TURN * 64) + pair * LANES, LANES), LANES)
            x = x_ref[0, :, lanes]
            top = skip_ref[:, lanes] * x[:half].astype(F32)
            bottom = skip_ref[:, lanes] * x[half:].astype(F32)
            for side in range(2):
                j = 2 * pair + side
                column = rolled[:, j : j + 1]
                cum_row = cum_rows[j : j + 1, :]
                step_row = step_rows[j : j + 1, :]
                own = jnp.where((lane < 64) == (side == 0), x, jnp.zeros_like(x))

                def mixing(r, c, masked):
                    diff = column[r] - cum_row[:, c]
                    if masked:
                        diff = jnp.where(causal, diff, -1e30)
                    return (scores[r, c] * jnp.exp(diff) * step_row[:, c]).astype(BF16)

                lo, hi = slice(0, half), slice(half, GROUP)
                top = top + dot(mixing(lo, lo, True), own[:half])
                bottom = bottom + dot(mixing(hi, lo, False), own[:half])
                bottom = bottom + dot(mixing(hi, hi, True), own[half:])
            y_ref[0, :half, lanes] = top
            y_ref[0, half:, lanes] = bottom


def inside(x, bc, raw, cum, step_bias, skip):
    s, length, width = x.shape
    rows = lambda n: pl.BlockSpec((1, GROUP, n), lambda i, j: (i, j, 0))
    return pl.pallas_call(
        inside_kernel,
        grid=(s, length // GROUP),
        in_specs=[
            rows(width), rows(bc.shape[-1]), rows(LANES), rows(LANES), whole(step_bias.shape),
            whole(skip.shape),
        ],
        out_specs=rows(width),
        out_shape=jax.ShapeDtypeStruct((s, length, width), F32),
        scratch_shapes=[
            pltpu.VMEM((LANES, GROUP), F32), pltpu.VMEM((LANES, GROUP), F32),
            pltpu.VMEM((GROUP, GROUP), F32),
        ],
        compiler_params=params(),
        name="inside",
        cost_estimate=pl.CostEstimate(flops=10_000_000_000, bytes_accessed=20_000_000, transcendentals=0),
    )(x, bc, raw, cum, step_bias, skip)


def product_kernel(
    rounded, index_ref, a_ref, w0, w1, w2, w3, w4, down_ref, up_ref, out_ref, full_ref, w_ref, sem, out_sem
):
    keep = pltpu.make_async_copy(w_ref, full_ref, out_sem)

    @pl.when((pl.program_id(0) == 0) & (pl.program_id(1) == 0))
    def _():
        assemble(index_ref[pl.num_programs(0)], (w0, w1, w2, w3, w4), w_ref, sem)
        keep.start()

    a = a_ref[0]
    up = up_ref[...].reshape(up_ref.shape[-2:]) if len(up_ref.shape) == 3 else up_ref[0, 0]
    if rounded:
        low = dot(a, down_ref[0]).astype(BF16)
        extra = dot(low, up)
    else:
        high, rest = split(dot_nt(a, down_ref[0]))
        extra = dot_nt(high, up) + dot_nt(rest, up)
    out_ref[0] = dot(a, w_ref[...]) + extra

    @pl.when((pl.program_id(0) == pl.num_programs(0) - 1) & (pl.program_id(1) == pl.num_programs(1) - 1))
    def _():
        keep.wait()


def product(index, a, w, down, up, rounded):
    s, length, depth = a.shape
    width = w[0].shape[1]
    tile = min(length, 2 * GROUP)
    down_spec = pl.BlockSpec((1,) + down.shape[1:], lambda i, j, idx: (idx[i], 0, 0))
    if rounded:
        up_spec = pl.BlockSpec((1, 1) + up.shape[2:], lambda i, j, idx: (idx[i], 0, 0, 0))
    else:
        up_spec = pl.BlockSpec((1,) + up.shape[1:], lambda i, j, idx: (idx[i], 0, 0))
    return pl.pallas_call(
        functools.partial(product_kernel, rounded),
        grid_spec=pltpu.PrefetchScalarGridSpec(
            num_scalar_prefetch=1,
            grid=(s, length // tile),
            in_specs=[
                pl.BlockSpec((1, tile, depth), lambda i, j, _: (i, j, 0)),
                *[ANYWHERE] * 5, down_spec, up_spec,
            ],
            out_specs=[pl.BlockSpec((1, tile, width), lambda i, j, _: (i, j, 0)), ANYWHERE],
            scratch_shapes=[
                pltpu.VMEM((depth, width), BF16), pltpu.SemaphoreType.DMA, pltpu.SemaphoreType.DMA,
            ],
        ),
        out_shape=[
            jax.ShapeDtypeStruct((s, length, width), F32), jax.ShapeDtypeStruct((depth, width), BF16)
        ],
        compiler_params=params(),
        name="product",
        cost_estimate=pl.CostEstimate(
            flops=2 * s * length * depth * width, bytes_accessed=15_000_000, transcendentals=0
        ),
    )(index, a, *w, down, up)


def gated_kernel(
    y_ref, bc_ref, cum_ref, loc_ref, in_ref, gate_ref, gn_ref, gain_ref, e_ref,
    mixer_ref, sums_ref, start_ref, entering,
):
    b = pl.program_id(1)
    states = bc_ref.shape[-1] // 2
    width = y_ref.shape[-1]
    cum = cum_ref[0]
    c_mat = bc_ref[0, :, states:]
    rise_high, rise_low = split(jnp.exp(cum))
    squares = jnp.zeros((GROUP, LANES), F32)
    crosses = jnp.zeros((GROUP, LANES), F32)

    for at in range(0, width, LANES):
        lanes = slice(at, at + LANES)
        table = e_ref[:, lanes]
        rise = dot(rise_high, table) + dot(rise_low, table)

        @pl.when(b == 0)
        def _():
            entering[:, lanes] = in_ref[0, :, lanes].astype(F32)

        own = jnp.where(b == 0, 0.0, loc_ref[0, 0, :, lanes])
        start = (entering[:, lanes] + own).astype(BF16)
        start_ref[0, 0, :, lanes] = start
        entering[:, lanes] = entering[:, lanes] * rise[GROUP - 1 :]
        mixer = y_ref[0, :, lanes] + dot(c_mat, start) * rise
        mixer_ref[0, :, lanes] = mixer
        gate = gate_ref[0, :, lanes]
        gated = mixer * (gate * sigmoid(gate))
        squares = squares + gated * gated
        crosses = crosses + gated * (gn_ref[0, :, lanes] * gain_ref[:, lanes])
    lane = lax.broadcasted_iota(jnp.int32, (GROUP, LANES), 1)
    square = jnp.sum(squares, axis=-1, keepdims=True)
    cross = jnp.sum(crosses, axis=-1, keepdims=True)
    both = jnp.where(lane == 0, square, jnp.where(lane == 1, cross, 0.0))
    sums_ref[0] = both.T[:HALO]


def gated(y, bc, cum, loc, came, gate, gn, gain, e):
    s, length, width = y.shape
    blocks = length // GROUP
    states = bc.shape[-1] // 2
    rows = lambda n: pl.BlockSpec((1, GROUP, n), lambda i, j: (i, j, 0))
    return pl.pallas_call(
        gated_kernel,
        grid=(s, blocks),
        in_specs=[
            rows(width), rows(2 * states), rows(LANES),
            pl.BlockSpec((1, 1, states, width), lambda i, j: (i, jnp.maximum(j - 1, 0), 0, 0)),
            pl.BlockSpec((1, states, width), lambda i, j: (i, 0, 0)),
            rows(width), rows(width), whole(gain.shape), whole(e.shape),
        ],
        out_specs=[
            rows(width),
            pl.BlockSpec((1, HALO, GROUP), lambda i, j: (i, 0, j)),
            pl.BlockSpec((1, 1, states, width), lambda i, j: (i, j, 0, 0)),
        ],
        out_shape=[
            jax.ShapeDtypeStruct((s, length, width), F32),
            jax.ShapeDtypeStruct((s, HALO, length), F32),
            jax.ShapeDtypeStruct((s, blocks, states, width), BF16),
        ],
        scratch_shapes=[pltpu.VMEM((states, width), F32)],
        compiler_params=params(),
        name="gated",
        cost_estimate=pl.CostEstimate(flops=500_000_000, bytes_accessed=30_000_000, transcendentals=0),
    )(y, bc, cum, loc, came, gate, gn, gain, e)


def turn_kernel(
    mixer_ref, gate_ref, gn_ref, sums_ref, other_ref, x_ref, bc_ref, cum_ref, start_ref, gain_ref,
    skip_ref, e_ref, et_ref,
    g_ref, gg_ref, nout_ref, fol_ref, pend_ref, gc_ref, row_ref, pending,
):
    j = pl.program_id(1)
    states = bc_ref.shape[-1] // 2
    width = x_ref.shape[-1]
    c_mat = bc_ref[0, :, states:]
    both = (sums_ref[0] + other_ref[0]).T
    scale = lax.rsqrt(both[:, 0:1] / MIXER_WIDTH + EPSILON)
    pull = scale * scale * scale * (both[:, 1:2] / MIXER_WIDTH)
    rise_high, rise_low = split(jnp.exp(cum_ref[0]))
    grad_c = jnp.zeros((GROUP, states), F32)
    row = jnp.zeros((GROUP, LANES), F32)
    for at in range(0, width, LANES):
        lanes = slice(at, at + LANES)
        table = e_ref[:, lanes]
        rise = dot(rise_high, table) + dot(rise_low, table)
        gate = gate_ref[0, :, lanes]
        mixer = mixer_ref[0, :, lanes]
        sig = sigmoid(gate)
        silu = gate * sig
        value = mixer * silu
        gain = gain_ref[:, lanes]
        nout_ref[0, :, lanes] = (value * scale * gain).astype(BF16)
        grad = scale * (gn_ref[0, :, lanes] * gain) - value * pull
        g = (grad * silu).astype(BF16)
        g_ref[0, :, lanes] = g
        gg_ref[0, :, lanes] = (grad * mixer * (sig * (1.0 + gate * (1.0 - sig)))).astype(BF16)
        gf = g.astype(F32)
        scaled = (gf * rise).astype(BF16)
        grad_c = grad_c + dot_nt(scaled, start_ref[0, 0, :, lanes])
        own = mixer - skip_ref[:, lanes] * x_ref[0, :, lanes].astype(F32)
        row = row + exact_dot(gf * own, et_ref[lanes, :])
        before = jnp.where(j == 0, 0.0, pending[:, lanes])
        fol_ref[0, 0, :, lanes] = before
        new = dot_tn(c_mat, scaled) + rise[GROUP - 1 :] * before
        pending[:, lanes] = new
        pend_ref[0, :, lanes] = new.astype(BF16)
    gc_ref[0] = grad_c
    row_ref[0] = row


def turn_back(mixer, gate, gn, sums, other, x, bc, cum, start, gain, skip, e, et):
    s, length, width = x.shape
    blocks = length // GROUP
    states = bc.shape[-1] // 2
    rows = lambda n: pl.BlockSpec((1, GROUP, n), lambda i, j: (i, blocks - 1 - j, 0))
    state = pl.BlockSpec((1, 1, states, width), lambda i, j: (i, blocks - 1 - j, 0, 0))
    sums_spec = pl.BlockSpec((1, HALO, GROUP), lambda i, j: (i, 0, blocks - 1 - j))
    out = lambda n, kind: jax.ShapeDtypeStruct((s, length, n), kind)
    return pl.pallas_call(
        turn_kernel,
        grid=(s, blocks),
        in_specs=[
            rows(width), rows(width), rows(width), sums_spec, sums_spec, rows(width),
            rows(2 * states), rows(LANES), state, whole(gain.shape), whole(skip.shape),
            whole(e.shape), whole(et.shape),
        ],
        out_specs=[
            rows(width), rows(width), rows(width), state,
            pl.BlockSpec((1, states, width), lambda i, j: (i, 0, 0)),
            rows(states), rows(LANES),
        ],
        out_shape=[
            out(width, BF16), out(width, BF16), out(width, BF16),
            jax.ShapeDtypeStruct((s, blocks, states, width), F32),
            jax.ShapeDtypeStruct((s, states, width), BF16),
            out(states, F32), out(LANES, F32),
        ],
        scratch_shapes=[pltpu.VMEM((states, width), F32)],
        compiler_params=params(),
        name="turn_back",
        cost_estimate=pl.CostEstimate(flops=2_000_000_000, bytes_accessed=35_000_000, transcendentals=0),
    )(mixer, gate, gn, sums, other, x, bc, cum, start, gain, skip, e, et)


def inside_back_kernel(
    x_ref, g_ref, bc_ref, raw_ref, cum_ref, step_bias_ref, et_ref,
    y_ref, gb_ref, gc_ref, direct_ref, cum_t, scores, grad_scores,
):
    states = bc_ref.shape[-1] // 2
    width = x_ref.shape[-1]
    cum = cum_ref[0]
    step = jax.nn.softplus(raw_ref[0] + step_bias_ref[...])
    cum_t[...] = cum.T
    b_mat = bc_ref[0, :, :states]
    c_mat = bc_ref[0, :, states:]
    scores[...] = dot_nt(b_mat, c_mat)
    grad_scores[...] = jnp.zeros_like(grad_scores)
    lane = lax.broadcasted_iota(jnp.int32, (GROUP, LANES), 1)
    causal = lax.broadcasted_iota(jnp.int32, (LANES, LANES), 0) <= lax.broadcasted_iota(
        jnp.int32, (LANES, LANES), 1
    )
    half = GROUP // 2
    direct_ref[0] = jnp.zeros((GROUP, LANES), F32)

    @pl.loop(0, width // 64 // TURN)
    def _(turn):
        shift = (LANES - TURN * turn) % LANES
        rolled = pltpu.roll(cum, shift, 1)
        rolled_step = pltpu.roll(step, shift, 1)
        cum_rows = cum_t[pl.ds(pl.multiple_of(turn * TURN, TURN), TURN), :]
        for pair in range(TURN // 2):
            at = pl.multiple_of(turn * (TURN * 64) + pair * LANES, LANES)
            lanes = pl.ds(at, LANES)
            x = x_ref[0, :, lanes]
            g = g_ref[0, :, lanes]
            top = jnp.zeros((half, LANES), F32)
            bottom = jnp.zeros((half, LANES), F32)
            for side in range(2):
                j = 2 * pair + side
                column = rolled[:, j : j + 1]
                step_column = rolled_step[:, j : j + 1]
                row = cum_rows[j : j + 1, :]
                own = jnp.where((lane < 64) == (side == 0), g, jnp.zeros_like(g))
                lo, hi = slice(0, half), slice(half, GROUP)

                def tile(r, c, masked):
                    diff = row[:, c] - column[r]
                    if masked:
                        diff = jnp.where(causal, diff, -1e30)
                    decay = jnp.exp(diff)
                    grad_mix = dot_nt(x[r], own[c])
                    grad_scores[r, c] += grad_mix * (decay * step_column[r])
                    return dot((scores[r, c] * decay).astype(BF16), own[c])

                top = top + tile(lo, lo, True) + tile(lo, hi, False)
                bottom = bottom + tile(hi, hi, True)
            y_ref[0, :half, lanes] = top
            y_ref[0, half:, lanes] = bottom
            et = et_ref[lanes, :]
            direct_ref[0, :half] += exact_dot(top * x[:half].astype(F32), et)
            direct_ref[0, half:] += exact_dot(bottom * x[half:].astype(F32), et)

    high, low = split(grad_scores[...])
    gb_ref[0] = dot(high, c_mat) + dot(low, c_mat)
    gc_ref[0] = dot_tn(high, b_mat) + dot_tn(low, b_mat)


def inside_back(x, g, bc, raw, cum, step_bias, et):
    s, length, width = x.shape
    states = bc.shape[-1] // 2
    rows = lambda n: pl.BlockSpec((1, GROUP, n), lambda i, j: (i, j, 0))
    out = lambda n: jax.ShapeDtypeStruct((s, length, n), F32)
    return pl.pallas_call(
        inside_back_kernel,
        grid=(s, length // GROUP),
        in_specs=[
            rows(width), rows(width), rows(2 * states), rows(LANES), rows(LANES),
            whole(step_bias.shape), whole(et.shape),
        ],
        out_specs=[rows(width), rows(states), rows(states), rows(LANES)],
        out_shape=[out(width), out(states), out(states), out(LANES)],
        scratch_shapes=[
            pltpu.VMEM((LANES, GROUP), F32), pltpu.VMEM((GROUP, GROUP), F32),
            pltpu.VMEM((GROUP, GROUP), F32),
        ],
        compiler_params=params(),
        name="inside_back",
        cost_estimate=pl.CostEstimate(flops=20_000_000_000, bytes_accessed=20_000_000, transcendentals=0),
    )(x, g, bc, raw, cum, step_bias, et)


def leave_kernel(
    tap_count, y_ref, x_ref, g_ref, bc_ref, raw_ref, cum_ref, conv_ref, before_ref, start_ref, fol_ref,
    later_ref, gb_ref, gc_ref, gc2_ref, row_ref, direct_ref, taps_ref, bias_ref, step_bias_ref,
    rate_ref, skip_ref, e_ref, et_ref,
    pack_ref, edge_ref, last_ref,
    ext, back, later,
):
    j = pl.program_id(1)
    width = x_ref.shape[-1]
    conv_width = conv_ref.shape[-1]
    states = (conv_width - width) // 2
    b_mat = bc_ref[0, :, :states]
    cum = cum_ref[0]
    raw = raw_ref[0] + step_bias_ref[...]
    step = jax.nn.softplus(raw)
    last = cum[GROUP - 1 :]
    fade = jnp.exp(last - cum)
    tail = fade * step
    tail_high, tail_low = split(tail)
    step_high, step_low = split(step)
    decay_high, decay_low = split(jnp.broadcast_to(jnp.exp(last), (HALO, LANES)))
    ext[:HALO] = before_ref[0, 0].astype(F32)
    ext[HALO:] = conv_ref[0].astype(F32)

    @pl.when(j == 0)
    def _():
        back[GROUP:] = jnp.zeros((HALO, conv_width), F32)

    @pl.when(j > 0)
    def _():
        back[GROUP:] = back[:HALO]

    grad_tail = jnp.zeros((GROUP, LANES), F32)
    grad_b = gb_ref[0]
    block_decay = jnp.zeros((HALO, LANES), F32)

    def through_conv(lanes, grad):
        value = conv_taps(ext, taps_ref, bias_ref, lanes, tap_count)
        back[:GROUP, lanes] = grad * silu_grad(value)
        total = jnp.zeros((GROUP, LANES), F32)
        for k in range(tap_count):
            ahead = tap_count - 1 - k
            total = total + taps_ref[k : k + 1, lanes] * back[ahead : ahead + GROUP, lanes]
        pack_ref[0, :, lanes] = total.astype(BF16)
        last_ref[0, :, lanes] = jnp.where(j == 0, total[GROUP - HALO :], last_ref[0, :, lanes])

    for at in range(0, width, LANES):
        lanes = slice(at, at + LANES)
        table = e_ref[:, lanes]
        et = et_ref[lanes, :]

        @pl.when(j == 0)
        def _():
            later[:, lanes] = later_ref[0, :, lanes].astype(F32)

        x = x_ref[0, :, lanes].astype(F32)
        whole_grad = later[:, lanes] + fol_ref[0, 0, :, lanes]
        fresh = whole_grad.astype(BF16)
        start = start_ref[0, 0, :, lanes].astype(F32)
        decay = (dot(decay_high, table) + dot(decay_low, table))[:1]
        later[:, lanes] = later[:, lanes] * decay
        product = jnp.sum(whole_grad * start, axis=0, keepdims=True)
        block_decay = block_decay + exact_dot(jnp.broadcast_to(product, (HALO, LANES)), et)
        tails = dot(tail_high, table) + dot(tail_low, table)
        steps = dot(step_high, table) + dot(step_low, table)
        by_b = dot(b_mat, fresh)
        weighted = (x * tails).astype(BF16)
        grad_b = grad_b + dot_nt(weighted, fresh)
        grad_tail = grad_tail + exact_dot(by_b * x, et)
        grad_x = (
            steps * y_ref[0, :, lanes]
            + skip_ref[:, lanes] * g_ref[0, :, lanes].astype(F32)
            + by_b * tails
        )
        through_conv(lanes, grad_x)
    through_conv(slice(width, width + states), grad_b)
    through_conv(slice(width + states, conv_width), gc_ref[0] + gc2_ref[0])

    direct = direct_ref[0]
    tail_pull = grad_tail * tail
    end_pull = jnp.sum(tail_pull, axis=0, keepdims=True) + block_decay[:1] * jnp.exp(last)
    at_end = lax.broadcasted_iota(jnp.int32, (GROUP, LANES), 0) == GROUP - 1
    grad_cum = row_ref[0] - step * direct - tail_pull + jnp.where(at_end, end_pull, 0.0)
    grad_step = direct + grad_tail * fade + running_sum(grad_cum, True) * rate_ref[...]
    lane = lax.broadcasted_iota(jnp.int32, (GROUP, LANES), 1)
    grad_raw = jnp.where(lane < width // 64, grad_step * sigmoid(raw), 0.0)
    pack_ref[0, :, conv_width:] = grad_raw.astype(BF16)

    rows = []
    for position in range(-HALO, 0):
        total = jnp.zeros((1, conv_width), F32)
        for k in range(tap_count):
            at = position + tap_count - 1 - k
            if at >= 0:
                total = total + taps_ref[k : k + 1, :] * back[at : at + 1, :]
        rows.append(total)
    edge_ref[0] = jnp.concatenate(rows, axis=0)


def leave(
    y, x, g, bc, raw, cum, conv, before, start, fol, later, gb, gc, gc2, row, direct, taps, bias,
    step_bias, rate, skip, e, et,
):
    s, length, width = x.shape
    conv_width = conv.shape[-1]
    blocks = length // GROUP
    states = bc.shape[-1] // 2
    rows = lambda n: pl.BlockSpec((1, GROUP, n), lambda i, j: (i, blocks - 1 - j, 0))
    state = pl.BlockSpec((1, 1, states, width), lambda i, j: (i, blocks - 1 - j, 0, 0))
    edge = pl.BlockSpec((1, HALO, conv_width), lambda i, j: (i, 0, 0))
    return pl.pallas_call(
        functools.partial(leave_kernel, 4),
        grid=(s, blocks),
        in_specs=[
            rows(width), rows(width), rows(width), rows(2 * states), rows(LANES), rows(LANES),
            rows(conv_width),
            pl.BlockSpec((1, 1, HALO, conv_width), lambda i, j: (i, blocks - 1 - j, 0, 0)),
            state, state, pl.BlockSpec((1, states, width), lambda i, j: (i, 0, 0)),
            rows(states), rows(states), rows(states), rows(LANES), rows(LANES),
            whole(taps.shape), whole(bias.shape), whole(step_bias.shape), whole(rate.shape),
            whole(skip.shape), whole(e.shape), whole(et.shape),
        ],
        out_specs=[rows(conv_width + LANES), edge, edge],
        out_shape=[
            jax.ShapeDtypeStruct((s, length, conv_width + LANES), BF16),
            jax.ShapeDtypeStruct((s, HALO, conv_width), F32),
            jax.ShapeDtypeStruct((s, HALO, conv_width), F32),
        ],
        scratch_shapes=[
            pltpu.VMEM((GROUP + HALO, conv_width), F32),
            pltpu.VMEM((GROUP + HALO, conv_width), F32),
            pltpu.VMEM((states, width), F32),
        ],
        compiler_params=params(),
        name="leave",
        cost_estimate=pl.CostEstimate(flops=2_000_000_000, bytes_accessed=40_000_000, transcendentals=0),
    )(
        y, x, g, bc, raw, cum, conv, before, start, fol, later, gb, gc, gc2, row, direct, taps, bias,
        step_bias, rate, skip, e, et,
    )


def chained(decay, own, axis, distance):
    leaving = own
    for _ in range(lax.axis_size(axis) - 1):
        came = shifted(leaving.astype(BF16), axis, distance)
        leaving = decay * came.astype(F32) + own
    return came


def by_adapter(per_slot, everyone):
    distance = 1
    while distance < lax.axis_size("ctx"):
        mine = per_slot.astype(BF16)
        per_slot = mine.astype(F32) + swapped(mine, "ctx", distance).astype(F32)
        distance *= 2
    slots = per_slot.astype(BF16)
    for distance in (1, 2):
        slots = jnp.concatenate([slots, swapped(slots, "dp", distance)])
    return jnp.einsum("sa,src->arc", everyone, slots, preferred_element_type=F32)


def partner_sum(value, kind):
    mine = value.astype(kind)
    return mine.astype(F32) + partner(mine, "tensor").astype(F32)


def on_device(
    tokens,
    cotangent,
    lengths,
    slot_adapter_index,
    input_norm_gain,
    gate_weight_matrix,
    inner_weight_matrix,
    state_map_weight,
    step_size_weight,
    output_projection_weight,
    inner_channel_taps,
    state_map_taps,
    inner_conv_bias,
    state_map_conv_bias,
    step_size_bias,
    log_decay_rate,
    head_skip_gain,
    gated_norm_gain,
    adapter_in_down_maps,
    adapter_in_up_maps,
    adapter_out_down_maps,
    adapter_out_up_maps,
):
    slot_count, length, model_width = tokens.shape
    width = gate_weight_matrix.shape[1]
    heads = step_size_bias.shape[0]
    head_dim = width // heads
    conv_width = width + state_map_weight.shape[1]
    taps_before = inner_channel_taps.shape[0] - 1
    adapter_set = adapter_in_down_maps.shape[0]
    rank = adapter_in_down_maps.shape[-1]
    spare = -heads % LANES
    rows = step_size_weight.shape[0]
    picks = jnp.broadcast_to(slot_adapter_index.astype(BF16)[None], (rows, slot_count))
    packed = jnp.concatenate(
        [
            inner_weight_matrix,
            state_map_weight,
            step_size_weight,
            jnp.zeros((rows, spare - slot_count), BF16),
            picks,
        ],
        axis=1,
    )
    halo = shifted(tokens[:, length - HALO :], "ctx", 1)
    packed_parts = rows_of_all(packed)
    out_mine, packed_parts = lax.optimization_barrier((output_projection_weight, packed_parts))
    out_parts = rows_of_all(out_mine)
    gate_mine, *arrived = lax.optimization_barrier((gate_weight_matrix, *out_parts[1:3]))
    out_parts = (out_parts[0], *arrived, *out_parts[3:])
    gate_parts = rows_of_all(gate_mine)
    all_slots = jnp.concatenate([part[0, -slot_count:] for part in packed_parts[:4]])
    everyone = (all_slots[:, None] == jnp.arange(adapter_set, dtype=jnp.int32).astype(BF16)[None, :]).astype(BF16)
    index = jnp.concatenate([slot_adapter_index, lax.axis_index("dp")[None].astype(jnp.int32)])
    places = lax.axis_index("ctx") * length + jnp.arange(length, dtype=jnp.int32)
    live_mask = (places[None, :] < lengths[:, None]).astype(F32)[..., None]
    selector = (
        slot_adapter_index[:, None] == jnp.arange(adapter_set, dtype=jnp.int32)[None, :]
    ).astype(BF16)

    head_of = jnp.arange(width, dtype=jnp.int32) // head_dim
    e = (jnp.arange(LANES, dtype=jnp.int32)[:, None] == head_of[None, :]).astype(BF16)
    et = (head_of[:, None] == jnp.arange(LANES, dtype=jnp.int32)[None, :]).astype(BF16)
    step_bias = jnp.pad(step_size_bias, (0, spare))[None]
    rate = jnp.pad(-jnp.exp(log_decay_rate), (0, spare))[None]
    skip = jnp.repeat(head_skip_gain, head_dim)[None]
    gain = gated_norm_gain[None]
    taps = jnp.concatenate([inner_channel_taps, state_map_taps], axis=1)
    conv_bias = jnp.concatenate([inner_conv_bias, state_map_conv_bias])[None]
    grad_branch = (cotangent.astype(F32) * live_mask).astype(BF16)

    normed, low_in, conv, x, bc, raw, cum, loc, before, packed_full = enter(
        index, tokens, halo, input_norm_gain[None], packed_parts, adapter_in_down_maps,
        adapter_in_up_maps, taps, conv_bias, step_bias, rate, e, width, conv_width,
    )
    device_decay = jnp.exp(jnp.sum(cum[:, GROUP - 1 :: GROUP, :heads], axis=1))
    device_decay = jnp.repeat(device_decay, head_dim, axis=1)[:, None, :]
    came = chained(device_decay, loc[:, -1], "ctx", 1)
    y = inside(x, bc, raw, cum, step_bias, skip)
    grad_normed, out_full = product(
        index, grad_branch, out_parts, adapter_out_up_maps, adapter_out_down_maps, False
    )
    gate, gate_full = product(index, normed, gate_parts, adapter_in_down_maps, adapter_in_up_maps, True)
    mixer, sums, start = gated(y, bc, cum, loc, came, gate, grad_normed, gain, e)
    other = partner(sums, "tensor")
    g, grad_gate, normed_out, fol, pend, grad_c2, row = turn_back(
        mixer, gate, grad_normed, sums, other, x, bc, cum, start, gain, skip, e, et
    )
    later = chained(device_decay, pend.astype(F32), "ctx", -1)

    out_down = jnp.einsum("sa,acr->scr", selector, adapter_out_down_maps, preferred_element_type=F32)
    out_down = out_down.astype(BF16)
    out_up = jnp.einsum("sa,ard->srd", selector, adapter_out_up_maps, preferred_element_type=F32)
    out_up = out_up.astype(BF16)
    partial_low = jnp.einsum("stc,scr->str", normed_out, out_down, preferred_element_type=F32)
    low_out = partner_sum(partial_low, F32).astype(BF16)
    partial_out = jnp.stack(
        [
            partner_sum(
                lax.dot_general(normed_out[s], out_full, (((1,), (1,)), ((), ())), preferred_element_type=F32),
                BF16,
            )
            for s in range(slot_count)
        ]
    )
    branch = partial_out + jnp.einsum("str,srd->std", low_out, out_up, preferred_element_type=F32)
    result = (tokens.astype(F32) + live_mask * branch).astype(BF16)
    grad_low_out = jnp.einsum("std,srd->str", grad_branch, out_up, preferred_element_type=F32)
    up_out_grad = jnp.einsum("str,std->srd", low_out, grad_branch, preferred_element_type=F32)
    down_out_grad = jnp.einsum(
        "str,stc->src", grad_low_out, normed_out.astype(F32), precision=lax.Precision.HIGH
    )
    in_down = jnp.einsum("sa,adr->sdr", selector, adapter_in_down_maps, preferred_element_type=F32)
    in_up = jnp.einsum("sa,aqrc->sqrc", selector, adapter_in_up_maps, preferred_element_type=F32)
    in_up = in_up.astype(BF16)
    up_gate_grad = jnp.einsum("str,stc->src", low_in, grad_gate, preferred_element_type=F32)
    early = by_adapter(jnp.concatenate([up_out_grad, down_out_grad, up_gate_grad], axis=1), everyone)
    nt = (((1,), (1,)), ((), ()))
    gate_low = jnp.einsum("stc,src->str", grad_gate, in_up[:, 0], preferred_element_type=F32)
    gate_in = [
        lax.dot_general(grad_gate[s], gate_full, nt, preferred_element_type=F32) for s in range(slot_count)
    ]
    gate_low, gate_in, later = lax.optimization_barrier((gate_low, gate_in, later))

    y_back, grad_b, grad_c, direct = inside_back(x, g, bc, raw, cum, step_bias, et)
    pack, edge, last = leave(
        y_back, x, g, bc, raw, cum, conv, before, start, fol, later, grad_b, grad_c, grad_c2, row,
        direct, taps, conv_bias, step_bias, rate, skip, e, et,
    )
    edge = shifted(edge[:, HALO - taps_before :].astype(BF16), "ctx", -1).astype(F32)
    last = last + jnp.pad(edge, ((0, 0), (HALO - taps_before, 0), (0, 0)))
    pack = lax.dynamic_update_slice(pack, last.astype(BF16), (0, length - HALO, 0))
    up_wide = jnp.pad(in_up[:, 1], ((0, 0), (0, 0), (0, pack.shape[-1] - width)))
    grad_low_sum = partner_sum(
        gate_low + jnp.einsum("stc,src->str", pack, up_wide, preferred_element_type=F32), F32
    )
    up_inner_grad = jnp.einsum("str,stc->src", low_in, pack, preferred_element_type=F32)[..., :width]
    down_in_grad = jnp.einsum(
        "str,std->srd", grad_low_sum, normed.astype(F32), precision=lax.Precision.HIGH
    )
    late = by_adapter(jnp.concatenate([up_inner_grad, down_in_grad], axis=1), everyone)
    partial_in = jnp.stack(
        [
            partner_sum(
                gate_in[s] + lax.dot_general(pack[s], packed_full, nt, preferred_element_type=F32), BF16
            )
            for s in range(slot_count)
        ]
    )
    grad_normed_in = partial_in + jnp.einsum(
        "str,sdr->std", grad_low_sum, in_down, precision=lax.Precision.HIGH
    )
    tok = tokens.astype(F32)
    in_scale = lax.rsqrt(jnp.mean(tok * tok, axis=-1, keepdims=True) + EPSILON)
    weighted = grad_normed_in * input_norm_gain
    grad_tokens = (
        cotangent.astype(F32)
        + in_scale * weighted
        - tok * in_scale**3 * jnp.mean(tok * weighted, axis=-1, keepdims=True)
    )
    return (
        result,
        grad_tokens,
        late[:, rank:].transpose(0, 2, 1),
        jnp.stack([early[:, 2 * rank :], late[:, :rank]], axis=1),
        early[:, rank : 2 * rank].transpose(0, 2, 1),
        early[:, :rank],
    )


def solution(mesh):
    in_specs = (
        P("dp", "ctx", None),
        P("dp", "ctx", None),
        P("dp"),
        P("dp"),
        P(),
        P("dp", "tensor"),
        P("dp", "tensor"),
        P("dp", None),
        P("dp", "tensor"),
        P("dp", "tensor"),
        P(None, "tensor"),
        P(),
        P("tensor"),
        P(),
        P("tensor"),
        P("tensor"),
        P("tensor"),
        P("tensor"),
        P(),
        P(None, None, None, "tensor"),
        P(None, "tensor", None),
        P(),
    )
    out_specs = (
        P("dp", "ctx", None),
        P("dp", "ctx", None),
        P(),
        P(None, None, None, "tensor"),
        P(None, "tensor", None),
        P(),
    )
    return jax.shard_map(
        on_device, mesh=mesh, in_specs=in_specs, out_specs=out_specs, check_vma=False
    )
```

```python
import functools

import jax
import jax.numpy as jnp
from jax import lax
from jax.experimental import pallas as pl
from jax.experimental.pallas import tpu as pltpu
from jax.sharding import PartitionSpec as P


DP, CTX, TENSOR = "dp", "ctx", "tensor"
MIXER_WIDTH = 3072
GROUP = 256
EPSILON = 1e-05
LANES = 128
WIDE = 512
HALO = 8
TURN = 8
F32 = jnp.float32
BF16 = jnp.bfloat16
VMEM_LIMIT = 60 * 1024 * 1024


def shifted(block, axis, distance):
    devices = range(lax.axis_size(axis))
    route = [(i - distance, i) for i in devices if i - distance in devices]
    return lax.ppermute(block, axis, route)


def partner(value, axis):
    size = lax.axis_size(axis)
    return lax.ppermute(value, axis, [(i, (i + 1) % size) for i in range(size)])


def swapped(value, axis, distance):
    return lax.ppermute(value, axis, [(i, i ^ distance) for i in range(lax.axis_size(axis))])


def rows_of_all(block):
    half = block.shape[0] // 2
    first = swapped(block, DP, 1)
    second = swapped(block, DP, 2)
    third = swapped(first[:half], DP, 2)
    fourth = swapped(second[half:], DP, 1)
    return block, first, second, third, fourth


def dot(a, b):
    return jnp.dot(a, b, preferred_element_type=F32)


def dot_nt(a, b):
    return lax.dot_general(a, b, (((1,), (1,)), ((), ())), preferred_element_type=F32)


def dot_tn(a, b):
    return lax.dot_general(a, b, (((0,), (0,)), ((), ())), preferred_element_type=F32)


def batched(a, b, x, y):
    return lax.dot_general(a, b, (((x,), (y,)), ((0,), (0,))), preferred_element_type=F32)


def rows_by_rows(a, b):
    return batched(a, b, 2, 2)


def rows_by_columns(a, b):
    return batched(a, b, 2, 1)


def over_positions(a, b):
    return batched(a, b, 1, 1)


def split(value):
    high = value.astype(BF16)
    return high, (value - high.astype(F32)).astype(BF16)


def exact_dot(value, table):
    high, low = split(value)
    return dot(high, table) + dot(low, table)


def sigmoid(value):
    return lax.logistic(value)


def silu_grad(value):
    g = sigmoid(value)
    return g * (1.0 + value * (1.0 - g))


def params(**more):
    return pltpu.CompilerParams(vmem_limit_bytes=VMEM_LIMIT, **more)


ANYWHERE = pl.BlockSpec(memory_space=pl.ANY)


def assemble(place, groups, table, sem):
    rows = groups[0][0].shape[0]
    half = rows // 2
    copies = []
    column = 0
    for parts in groups:
        columns = pl.ds(column, parts[0].shape[1])
        column += parts[0].shape[1]
        for step, first, part in zip((0, 1, 2, 3, 3), (0, 0, 0, 0, half), parts):
            at = pl.ds(pl.multiple_of((place ^ step) * rows + first, half), part.shape[0])
            copies.append(pltpu.make_async_copy(part, table.at[at, columns], sem))
    for copy in copies:
        copy.start()
    for copy in copies:
        copy.wait()


def whole(shape):
    return pl.BlockSpec(shape, lambda *_: (0,) * len(shape))


def running_sum(value, backwards=False):
    rows = value.shape[0]
    i = lax.broadcasted_iota(jnp.int32, (rows, rows), 0)
    j = lax.broadcasted_iota(jnp.int32, (rows, rows), 1)
    table = jnp.where(i <= j if backwards else i >= j, 1.0, 0.0).astype(F32)
    return jnp.dot(table, value, precision=lax.Precision.HIGHEST, preferred_element_type=F32)


def conv_taps(ext_ref, taps_ref, bias_ref, lanes, tap_count):
    value = jnp.zeros((GROUP, LANES), F32) + bias_ref[:, lanes]
    for k in range(tap_count):
        start = HALO - (tap_count - 1) + k
        value = value + taps_ref[k : k + 1, lanes] * ext_ref[start : start + GROUP, lanes]
    return value


def enter_kernel(
    tap_count, index_ref, tok_ref, halo_ref, gain_ref, w0, w1, w2, w3, w4, v0, v1, v2, v3, v4,
    down_ref, up_ref, taps_ref,
    bias_ref, step_bias_ref, rate_ref, e_ref,
    normed_ref, low_ref, conv_ref, x_ref, bc_ref, raw_ref, cum_ref, loc_ref, before_ref, full_ref,
    ext, state, w_ref, sem, out_sem,
):
    b = pl.program_id(1)
    keep = pltpu.make_async_copy(w_ref, full_ref, out_sem)

    @pl.when((pl.program_id(0) == 0) & (b == 0))
    def _():
        assemble(index_ref[pl.num_programs(0)], [(w0, w1, w2, w3, w4), (v0, v1, v2, v3, v4)], w_ref, sem)
        keep.start()

    width = x_ref.shape[-1]
    conv_width = conv_ref.shape[-1]

    def project(tok, rows):
        tok = tok.astype(F32)
        scale = lax.rsqrt(jnp.mean(tok * tok, axis=-1, keepdims=True) + EPSILON)
        normed = (tok * scale * gain_ref[...]).astype(BF16)
        low = dot(normed, down_ref[0]).astype(BF16)
        for at in range(0, width, WIDE):
            columns = slice(at, at + WIDE)
            inner = dot(normed, w_ref[:, columns]) + dot(low, up_ref[0, 1, :, columns])
            ext[rows, columns] = inner.astype(BF16).astype(F32)
        rest = dot(normed, w_ref[:, width:])
        ext[rows, width:] = rest[:, : conv_width - width].astype(BF16).astype(F32)
        return normed, low, rest

    @pl.when(b == 0)
    def _():
        project(halo_ref[0], slice(0, HALO))
        state[...] = jnp.zeros_like(state)

    @pl.when(b > 0)
    def _():
        ext[:HALO] = ext[GROUP:]

    before_ref[0, 0] = ext[:HALO].astype(BF16)
    normed, low, rest = project(tok_ref[0], slice(HALO, HALO + GROUP))
    normed_ref[0] = normed
    low_ref[0] = low
    conv_ref[0] = ext[HALO:].astype(BF16)
    raw = rest[:, conv_width - width :]
    raw_ref[0] = raw
    step = jax.nn.softplus(raw + step_bias_ref[...])
    cum = running_sum(step * rate_ref[...])
    cum_ref[0] = cum
    last = cum[GROUP - 1 :]
    tail = jnp.exp(last - cum) * step

    for at in range(width, conv_width, LANES):
        lanes = slice(at, at + LANES)
        value = conv_taps(ext, taps_ref, bias_ref, lanes, tap_count)
        bc_ref[0, :, at - width : at - width + LANES] = (value * sigmoid(value)).astype(BF16)
    b_mat = bc_ref[0, :, : bc_ref.shape[-1] // 2]
    tail_high, tail_low = split(tail)
    decay_high, decay_low = split(jnp.broadcast_to(jnp.exp(last), (HALO, LANES)))
    for at in range(0, width, LANES):
        lanes = slice(at, at + LANES)
        value = conv_taps(ext, taps_ref, bias_ref, lanes, tap_count)
        x = (value * sigmoid(value)).astype(BF16)
        x_ref[0, :, lanes] = x
        table = e_ref[:, lanes]
        weighted = (x.astype(F32) * (dot(tail_high, table) + dot(tail_low, table))).astype(BF16)
        decay = (dot(decay_high, table) + dot(decay_low, table))[:1]
        new = decay * state[:, lanes] + dot_tn(b_mat, weighted)
        state[:, lanes] = new
        loc_ref[0, 0, :, lanes] = new

    @pl.when((pl.program_id(0) == pl.num_programs(0) - 1) & (b == pl.num_programs(1) - 1))
    def _():
        keep.wait()


def enter(index, tokens, halo, gain, w, down, up, taps, bias, step_bias, rate, e, width, conv_width):
    s, length, model = tokens.shape
    blocks = length // GROUP
    rank = down.shape[-1]
    states = (conv_width - width) // 2
    full_width = w[0].shape[1] + w[5].shape[1]
    rows = lambda n: pl.BlockSpec((1, GROUP, n), lambda i, j, _: (i, j, 0))
    out = lambda n, kind: jax.ShapeDtypeStruct((s, length, n), kind)
    return pl.pallas_call(
        functools.partial(enter_kernel, 4),
        grid_spec=pltpu.PrefetchScalarGridSpec(
            num_scalar_prefetch=1,
            grid=(s, blocks),
            in_specs=[
                rows(model),
                pl.BlockSpec((1, HALO, model), lambda i, j, _: (i, 0, 0)),
                whole(gain.shape),
                *[ANYWHERE] * 10,
                pl.BlockSpec((1, model, rank), lambda i, j, idx: (idx[i], 0, 0)),
                pl.BlockSpec((1, 2, rank, width), lambda i, j, idx: (idx[i], 0, 0, 0)),
                whole(taps.shape),
                whole(bias.shape),
                whole(step_bias.shape),
                whole(rate.shape),
                whole(e.shape),
            ],
            out_specs=[
                rows(model), rows(rank), rows(conv_width), rows(width), rows(2 * states),
                rows(LANES), rows(LANES),
                pl.BlockSpec((1, 1, states, width), lambda i, j, _: (i, j, 0, 0)),
                pl.BlockSpec((1, 1, HALO, conv_width), lambda i, j, _: (i, j, 0, 0)),
                ANYWHERE,
            ],
            scratch_shapes=[
                pltpu.VMEM((GROUP + HALO, conv_width), F32),
                pltpu.VMEM((states, width), F32),
                pltpu.VMEM((model, full_width), BF16),
                pltpu.SemaphoreType.DMA,
                pltpu.SemaphoreType.DMA,
            ],
        ),
        out_shape=[
            out(model, BF16), out(rank, BF16), out(conv_width, BF16), out(width, BF16),
            out(2 * states, BF16), out(LANES, F32), out(LANES, F32),
            jax.ShapeDtypeStruct((s, blocks, states, width), F32),
            jax.ShapeDtypeStruct((s, blocks, HALO, conv_width), BF16),
            jax.ShapeDtypeStruct((model, full_width), BF16),
        ],
        compiler_params=params(),
        name="enter",
        cost_estimate=pl.CostEstimate(flops=15_000_000_000, bytes_accessed=30_000_000, transcendentals=0),
    )(index, tokens, halo, gain, *w, down, up, taps, bias, step_bias, rate, e)


def inside_kernel(x_ref, bc_ref, raw_ref, cum_ref, step_bias_ref, skip_ref, y_ref, cum_t, step_t, scores):
    states = bc_ref.shape[-1] // 2
    heads_at = x_ref.shape[-1] // 64
    cum = cum_ref[0]
    step = jax.nn.softplus(raw_ref[0] + step_bias_ref[...])
    cum_t[...] = cum.T
    step_t[...] = step.T
    scores[...] = dot_nt(bc_ref[0, :, states:], bc_ref[0, :, :states])
    lane = lax.broadcasted_iota(jnp.int32, (GROUP, LANES), 1)
    causal = lax.broadcasted_iota(jnp.int32, (LANES, LANES), 0) >= lax.broadcasted_iota(
        jnp.int32, (LANES, LANES), 1
    )
    half = GROUP // 2

    @pl.loop(0, heads_at // TURN)
    def _(turn):
        rolled = pltpu.roll(cum, (LANES - TURN * turn) % LANES, 1)
        rows = pl.ds(pl.multiple_of(turn * TURN, TURN), TURN)
        cum_rows = cum_t[rows, :]
        step_rows = step_t[rows, :]
        for pair in range(TURN // 2):
            lanes = pl.ds(pl.multiple_of(turn * (TURN * 64) + pair * LANES, LANES), LANES)
            x = x_ref[0, :, lanes]
            top = skip_ref[:, lanes] * x[:half].astype(F32)
            bottom = skip_ref[:, lanes] * x[half:].astype(F32)
            for side in range(2):
                j = 2 * pair + side
                column = rolled[:, j : j + 1]
                cum_row = cum_rows[j : j + 1, :]
                step_row = step_rows[j : j + 1, :]
                own = jnp.where((lane < 64) == (side == 0), x, jnp.zeros_like(x))

                def mixing(r, c, masked):
                    diff = column[r] - cum_row[:, c]
                    if masked:
                        diff = jnp.where(causal, diff, -1e30)
                    return (scores[r, c] * jnp.exp(diff) * step_row[:, c]).astype(BF16)

                lo, hi = slice(0, half), slice(half, GROUP)
                top = top + dot(mixing(lo, lo, True), own[:half])
                bottom = bottom + dot(mixing(hi, lo, False), own[:half])
                bottom = bottom + dot(mixing(hi, hi, True), own[half:])
            y_ref[0, :half, lanes] = top
            y_ref[0, half:, lanes] = bottom


def inside(x, bc, raw, cum, step_bias, skip):
    s, length, width = x.shape
    rows = lambda n: pl.BlockSpec((1, GROUP, n), lambda i, j: (i, j, 0))
    return pl.pallas_call(
        inside_kernel,
        grid=(s, length // GROUP),
        in_specs=[
            rows(width), rows(bc.shape[-1]), rows(LANES), rows(LANES), whole(step_bias.shape),
            whole(skip.shape),
        ],
        out_specs=rows(width),
        out_shape=jax.ShapeDtypeStruct((s, length, width), F32),
        scratch_shapes=[
            pltpu.VMEM((LANES, GROUP), F32), pltpu.VMEM((LANES, GROUP), F32),
            pltpu.VMEM((GROUP, GROUP), F32),
        ],
        compiler_params=params(),
        name="inside",
        cost_estimate=pl.CostEstimate(flops=10_000_000_000, bytes_accessed=20_000_000, transcendentals=0),
    )(x, bc, raw, cum, step_bias, skip)


def product_kernel(
    index_ref, a_ref, low_ref, w0, w1, w2, w3, w4, up_ref, out_ref, full_ref, w_ref, sem, out_sem
):
    keep = pltpu.make_async_copy(w_ref, full_ref, out_sem)

    @pl.when((pl.program_id(0) == 0) & (pl.program_id(1) == 0))
    def _():
        assemble(index_ref[pl.num_programs(0)], [(w0, w1, w2, w3, w4)], w_ref, sem)
        keep.start()

    a = a_ref[0]
    low = low_ref[0]
    for at in range(0, out_ref.shape[-1], WIDE):
        columns = slice(at, at + WIDE)
        out_ref[0, :, columns] = dot(a, w_ref[:, columns]) + dot(low, up_ref[0, :, columns])

    @pl.when((pl.program_id(0) == pl.num_programs(0) - 1) & (pl.program_id(1) == pl.num_programs(1) - 1))
    def _():
        keep.wait()


def product(index, a, low, w, up):
    s, length, depth = a.shape
    width = w[0].shape[1]
    tile = min(length, 2 * GROUP)
    return pl.pallas_call(
        product_kernel,
        grid_spec=pltpu.PrefetchScalarGridSpec(
            num_scalar_prefetch=1,
            grid=(s, length // tile),
            in_specs=[
                pl.BlockSpec((1, tile, depth), lambda i, j, _: (i, j, 0)),
                pl.BlockSpec((1, tile, low.shape[-1]), lambda i, j, _: (i, j, 0)),
                *[ANYWHERE] * 5,
                pl.BlockSpec((1,) + up.shape[1:], lambda i, j, _: (i, 0, 0)),
            ],
            out_specs=[pl.BlockSpec((1, tile, width), lambda i, j, _: (i, j, 0)), ANYWHERE],
            scratch_shapes=[
                pltpu.VMEM((depth, width), BF16), pltpu.SemaphoreType.DMA, pltpu.SemaphoreType.DMA,
            ],
        ),
        out_shape=[
            jax.ShapeDtypeStruct((s, length, width), F32), jax.ShapeDtypeStruct((depth, width), BF16)
        ],
        compiler_params=params(),
        name="product",
        cost_estimate=pl.CostEstimate(
            flops=2 * s * length * depth * width, bytes_accessed=15_000_000, transcendentals=0
        ),
    )(index, a, low, *w, up)


def gated_kernel(
    y_ref, bc_ref, cum_ref, loc_ref, in_ref, gate_ref, gn_ref, gain_ref, e_ref,
    mixer_ref, sums_ref, start_ref, entering,
):
    b = pl.program_id(1)
    states = bc_ref.shape[-1] // 2
    width = y_ref.shape[-1]
    cum = cum_ref[0]
    c_mat = bc_ref[0, :, states:]
    rise_high, rise_low = split(jnp.exp(cum))
    squares = jnp.zeros((GROUP, LANES), F32)
    crosses = jnp.zeros((GROUP, LANES), F32)

    for at in range(0, width, LANES):
        lanes = slice(at, at + LANES)
        table = e_ref[:, lanes]
        rise = dot(rise_high, table) + dot(rise_low, table)

        @pl.when(b == 0)
        def _():
            entering[:, lanes] = in_ref[0, :, lanes].astype(F32)

        own = jnp.where(b == 0, 0.0, loc_ref[0, 0, :, lanes])
        start = (entering[:, lanes] + own).astype(BF16)
        start_ref[0, 0, :, lanes] = start
        entering[:, lanes] = entering[:, lanes] * rise[GROUP - 1 :]
        mixer = y_ref[0, :, lanes] + dot(c_mat, start) * rise
        mixer_ref[0, :, lanes] = mixer
        gate = gate_ref[0, :, lanes]
        gated = mixer * (gate * sigmoid(gate))
        squares = squares + gated * gated
        crosses = crosses + gated * (gn_ref[0, :, lanes] * gain_ref[:, lanes])
    lane = lax.broadcasted_iota(jnp.int32, (GROUP, LANES), 1)
    square = jnp.sum(squares, axis=-1, keepdims=True)
    cross = jnp.sum(crosses, axis=-1, keepdims=True)
    both = jnp.where(lane == 0, square, jnp.where(lane == 1, cross, 0.0))
    sums_ref[0] = both.T[:HALO]


def gated(y, bc, cum, loc, came, gate, gn, gain, e):
    s, length, width = y.shape
    blocks = length // GROUP
    states = bc.shape[-1] // 2
    rows = lambda n: pl.BlockSpec((1, GROUP, n), lambda i, j: (i, j, 0))
    return pl.pallas_call(
        gated_kernel,
        grid=(s, blocks),
        in_specs=[
            rows(width), rows(2 * states), rows(LANES),
            pl.BlockSpec((1, 1, states, width), lambda i, j: (i, jnp.maximum(j - 1, 0), 0, 0)),
            pl.BlockSpec((1, states, width), lambda i, j: (i, 0, 0)),
            rows(width), rows(width), whole(gain.shape), whole(e.shape),
        ],
        out_specs=[
            rows(width),
            pl.BlockSpec((1, HALO, GROUP), lambda i, j: (i, 0, j)),
            pl.BlockSpec((1, 1, states, width), lambda i, j: (i, j, 0, 0)),
        ],
        out_shape=[
            jax.ShapeDtypeStruct((s, length, width), F32),
            jax.ShapeDtypeStruct((s, HALO, length), F32),
            jax.ShapeDtypeStruct((s, blocks, states, width), BF16),
        ],
        scratch_shapes=[pltpu.VMEM((states, width), F32)],
        compiler_params=params(),
        name="gated",
        cost_estimate=pl.CostEstimate(flops=500_000_000, bytes_accessed=30_000_000, transcendentals=0),
    )(y, bc, cum, loc, came, gate, gn, gain, e)


def turn_kernel(
    mixer_ref, gate_ref, gn_ref, sums_ref, other_ref, x_ref, bc_ref, cum_ref, start_ref, gain_ref,
    skip_ref, e_ref, et_ref,
    g_ref, gg_ref, nout_ref, fol_ref, pend_ref, gc_ref, row_ref, pending,
):
    j = pl.program_id(1)
    states = bc_ref.shape[-1] // 2
    width = x_ref.shape[-1]
    c_mat = bc_ref[0, :, states:]
    both = (sums_ref[0] + other_ref[0]).T
    scale = lax.rsqrt(both[:, 0:1] / MIXER_WIDTH + EPSILON)
    pull = scale * scale * scale * (both[:, 1:2] / MIXER_WIDTH)
    rise_high, rise_low = split(jnp.exp(cum_ref[0]))
    grad_c = jnp.zeros((GROUP, states), F32)
    row = jnp.zeros((GROUP, LANES), F32)
    for at in range(0, width, LANES):
        lanes = slice(at, at + LANES)
        table = e_ref[:, lanes]
        rise = dot(rise_high, table) + dot(rise_low, table)
        gate = gate_ref[0, :, lanes]
        mixer = mixer_ref[0, :, lanes]
        sig = sigmoid(gate)
        silu = gate * sig
        value = mixer * silu
        gain = gain_ref[:, lanes]
        nout_ref[0, :, lanes] = (value * scale * gain).astype(BF16)
        grad = scale * (gn_ref[0, :, lanes] * gain) - value * pull
        g = (grad * silu).astype(BF16)
        g_ref[0, :, lanes] = g
        gg_ref[0, :, lanes] = (grad * mixer * (sig * (1.0 + gate * (1.0 - sig)))).astype(BF16)
        gf = g.astype(F32)
        scaled = (gf * rise).astype(BF16)
        grad_c = grad_c + dot_nt(scaled, start_ref[0, 0, :, lanes])
        own = mixer - skip_ref[:, lanes] * x_ref[0, :, lanes].astype(F32)
        row = row + exact_dot(gf * own, et_ref[lanes, :])
        before = jnp.where(j == 0, 0.0, pending[:, lanes])
        fol_ref[0, 0, :, lanes] = before
        new = dot_tn(c_mat, scaled) + rise[GROUP - 1 :] * before
        pending[:, lanes] = new
        pend_ref[0, :, lanes] = new.astype(BF16)
    gc_ref[0] = grad_c
    row_ref[0] = row


def turn_back(mixer, gate, gn, sums, other, x, bc, cum, start, gain, skip, e, et):
    s, length, width = x.shape
    blocks = length // GROUP
    states = bc.shape[-1] // 2
    rows = lambda n: pl.BlockSpec((1, GROUP, n), lambda i, j: (i, blocks - 1 - j, 0))
    state = pl.BlockSpec((1, 1, states, width), lambda i, j: (i, blocks - 1 - j, 0, 0))
    sums_spec = pl.BlockSpec((1, HALO, GROUP), lambda i, j: (i, 0, blocks - 1 - j))
    out = lambda n, kind: jax.ShapeDtypeStruct((s, length, n), kind)
    return pl.pallas_call(
        turn_kernel,
        grid=(s, blocks),
        in_specs=[
            rows(width), rows(width), rows(width), sums_spec, sums_spec, rows(width),
            rows(2 * states), rows(LANES), state, whole(gain.shape), whole(skip.shape),
            whole(e.shape), whole(et.shape),
        ],
        out_specs=[
            rows(width), rows(width), rows(width), state,
            pl.BlockSpec((1, states, width), lambda i, j: (i, 0, 0)),
            rows(states), rows(LANES),
        ],
        out_shape=[
            out(width, BF16), out(width, BF16), out(width, BF16),
            jax.ShapeDtypeStruct((s, blocks, states, width), F32),
            jax.ShapeDtypeStruct((s, states, width), BF16),
            out(states, F32), out(LANES, F32),
        ],
        scratch_shapes=[pltpu.VMEM((states, width), F32)],
        compiler_params=params(),
        name="turn_back",
        cost_estimate=pl.CostEstimate(flops=2_000_000_000, bytes_accessed=35_000_000, transcendentals=0),
    )(mixer, gate, gn, sums, other, x, bc, cum, start, gain, skip, e, et)


def inside_back_kernel(
    x_ref, g_ref, bc_ref, raw_ref, cum_ref, step_bias_ref, et_ref,
    y_ref, gb_ref, gc_ref, direct_ref, cum_t, scores, grad_scores,
):
    states = bc_ref.shape[-1] // 2
    width = x_ref.shape[-1]
    cum = cum_ref[0]
    step = jax.nn.softplus(raw_ref[0] + step_bias_ref[...])
    cum_t[...] = cum.T
    b_mat = bc_ref[0, :, :states]
    c_mat = bc_ref[0, :, states:]
    scores[...] = dot_nt(b_mat, c_mat)
    grad_scores[...] = jnp.zeros_like(grad_scores)
    lane = lax.broadcasted_iota(jnp.int32, (GROUP, LANES), 1)
    causal = lax.broadcasted_iota(jnp.int32, (LANES, LANES), 0) <= lax.broadcasted_iota(
        jnp.int32, (LANES, LANES), 1
    )
    half = GROUP // 2
    direct_ref[0] = jnp.zeros((GROUP, LANES), F32)

    @pl.loop(0, width // 64 // TURN)
    def _(turn):
        shift = (LANES - TURN * turn) % LANES
        rolled = pltpu.roll(cum, shift, 1)
        rolled_step = pltpu.roll(step, shift, 1)
        cum_rows = cum_t[pl.ds(pl.multiple_of(turn * TURN, TURN), TURN), :]
        for pair in range(TURN // 2):
            at = pl.multiple_of(turn * (TURN * 64) + pair * LANES, LANES)
            lanes = pl.ds(at, LANES)
            x = x_ref[0, :, lanes]
            g = g_ref[0, :, lanes]
            top = jnp.zeros((half, LANES), F32)
            bottom = jnp.zeros((half, LANES), F32)
            for side in range(2):
                j = 2 * pair + side
                column = rolled[:, j : j + 1]
                step_column = rolled_step[:, j : j + 1]
                row = cum_rows[j : j + 1, :]
                own = jnp.where((lane < 64) == (side == 0), g, jnp.zeros_like(g))
                lo, hi = slice(0, half), slice(half, GROUP)

                def tile(r, c, masked):
                    diff = row[:, c] - column[r]
                    if masked:
                        diff = jnp.where(causal, diff, -1e30)
                    decay = jnp.exp(diff)
                    grad_mix = dot_nt(x[r], own[c])
                    grad_scores[r, c] += grad_mix * (decay * step_column[r])
                    return dot((scores[r, c] * decay).astype(BF16), own[c])

                top = top + tile(lo, lo, True) + tile(lo, hi, False)
                bottom = bottom + tile(hi, hi, True)
            y_ref[0, :half, lanes] = top
            y_ref[0, half:, lanes] = bottom
            et = et_ref[lanes, :]
            direct_ref[0, :half] += exact_dot(top * x[:half].astype(F32), et)
            direct_ref[0, half:] += exact_dot(bottom * x[half:].astype(F32), et)

    high, low = split(grad_scores[...])
    gb_ref[0] = dot(high, c_mat) + dot(low, c_mat)
    gc_ref[0] = dot_tn(high, b_mat) + dot_tn(low, b_mat)


def inside_back(x, g, bc, raw, cum, step_bias, et):
    s, length, width = x.shape
    states = bc.shape[-1] // 2
    rows = lambda n: pl.BlockSpec((1, GROUP, n), lambda i, j: (i, j, 0))
    out = lambda n: jax.ShapeDtypeStruct((s, length, n), F32)
    return pl.pallas_call(
        inside_back_kernel,
        grid=(s, length // GROUP),
        in_specs=[
            rows(width), rows(width), rows(2 * states), rows(LANES), rows(LANES),
            whole(step_bias.shape), whole(et.shape),
        ],
        out_specs=[rows(width), rows(states), rows(states), rows(LANES)],
        out_shape=[out(width), out(states), out(states), out(LANES)],
        scratch_shapes=[
            pltpu.VMEM((LANES, GROUP), F32), pltpu.VMEM((GROUP, GROUP), F32),
            pltpu.VMEM((GROUP, GROUP), F32),
        ],
        compiler_params=params(),
        name="inside_back",
        cost_estimate=pl.CostEstimate(flops=20_000_000_000, bytes_accessed=20_000_000, transcendentals=0),
    )(x, g, bc, raw, cum, step_bias, et)


def leave_kernel(
    tap_count, y_ref, x_ref, g_ref, bc_ref, raw_ref, cum_ref, conv_ref, before_ref, start_ref, fol_ref,
    later_ref, gb_ref, gc_ref, gc2_ref, row_ref, direct_ref, taps_ref, bias_ref, step_bias_ref,
    rate_ref, skip_ref, e_ref, et_ref,
    pack_ref, edge_ref, last_ref,
    ext, back, later,
):
    j = pl.program_id(1)
    width = x_ref.shape[-1]
    conv_width = conv_ref.shape[-1]
    states = (conv_width - width) // 2
    b_mat = bc_ref[0, :, :states]
    cum = cum_ref[0]
    raw = raw_ref[0] + step_bias_ref[...]
    step = jax.nn.softplus(raw)
    last = cum[GROUP - 1 :]
    fade = jnp.exp(last - cum)
    tail = fade * step
    tail_high, tail_low = split(tail)
    step_high, step_low = split(step)
    decay_high, decay_low = split(jnp.broadcast_to(jnp.exp(last), (HALO, LANES)))
    ext[:HALO] = before_ref[0, 0].astype(F32)
    ext[HALO:] = conv_ref[0].astype(F32)

    @pl.when(j == 0)
    def _():
        back[GROUP:] = jnp.zeros((HALO, conv_width), F32)

    @pl.when(j > 0)
    def _():
        back[GROUP:] = back[:HALO]

    grad_tail = jnp.zeros((GROUP, LANES), F32)
    grad_b = gb_ref[0]
    block_decay = jnp.zeros((HALO, LANES), F32)

    def through_conv(lanes, grad):
        value = conv_taps(ext, taps_ref, bias_ref, lanes, tap_count)
        back[:GROUP, lanes] = grad * silu_grad(value)
        total = jnp.zeros((GROUP, LANES), F32)
        for k in range(tap_count):
            ahead = tap_count - 1 - k
            total = total + taps_ref[k : k + 1, lanes] * back[ahead : ahead + GROUP, lanes]
        pack_ref[0, :, lanes] = total.astype(BF16)
        last_ref[0, :, lanes] = jnp.where(j == 0, total[GROUP - HALO :], last_ref[0, :, lanes])

    for at in range(0, width, LANES):
        lanes = slice(at, at + LANES)
        table = e_ref[:, lanes]
        et = et_ref[lanes, :]

        @pl.when(j == 0)
        def _():
            later[:, lanes] = later_ref[0, :, lanes].astype(F32)

        x = x_ref[0, :, lanes].astype(F32)
        whole_grad = later[:, lanes] + fol_ref[0, 0, :, lanes]
        fresh = whole_grad.astype(BF16)
        start = start_ref[0, 0, :, lanes].astype(F32)
        decay = (dot(decay_high, table) + dot(decay_low, table))[:1]
        later[:, lanes] = later[:, lanes] * decay
        product = jnp.sum(whole_grad * start, axis=0, keepdims=True)
        block_decay = block_decay + exact_dot(jnp.broadcast_to(product, (HALO, LANES)), et)
        tails = dot(tail_high, table) + dot(tail_low, table)
        steps = dot(step_high, table) + dot(step_low, table)
        by_b = dot(b_mat, fresh)
        weighted = (x * tails).astype(BF16)
        grad_b = grad_b + dot_nt(weighted, fresh)
        grad_tail = grad_tail + exact_dot(by_b * x, et)
        grad_x = (
            steps * y_ref[0, :, lanes]
            + skip_ref[:, lanes] * g_ref[0, :, lanes].astype(F32)
            + by_b * tails
        )
        through_conv(lanes, grad_x)
    through_conv(slice(width, width + states), grad_b)
    through_conv(slice(width + states, conv_width), gc_ref[0] + gc2_ref[0])

    direct = direct_ref[0]
    tail_pull = grad_tail * tail
    end_pull = jnp.sum(tail_pull, axis=0, keepdims=True) + block_decay[:1] * jnp.exp(last)
    at_end = lax.broadcasted_iota(jnp.int32, (GROUP, LANES), 0) == GROUP - 1
    grad_cum = row_ref[0] - step * direct - tail_pull + jnp.where(at_end, end_pull, 0.0)
    grad_step = direct + grad_tail * fade + running_sum(grad_cum, True) * rate_ref[...]
    lane = lax.broadcasted_iota(jnp.int32, (GROUP, LANES), 1)
    grad_raw = jnp.where(lane < width // 64, grad_step * sigmoid(raw), 0.0)
    pack_ref[0, :, conv_width:] = grad_raw.astype(BF16)

    rows = []
    for position in range(-HALO, 0):
        total = jnp.zeros((1, conv_width), F32)
        for k in range(tap_count):
            at = position + tap_count - 1 - k
            if at >= 0:
                total = total + taps_ref[k : k + 1, :] * back[at : at + 1, :]
        rows.append(total)
    edge_ref[0] = jnp.concatenate(rows, axis=0)


def leave(
    y, x, g, bc, raw, cum, conv, before, start, fol, later, gb, gc, gc2, row, direct, taps, bias,
    step_bias, rate, skip, e, et,
):
    s, length, width = x.shape
    conv_width = conv.shape[-1]
    blocks = length // GROUP
    states = bc.shape[-1] // 2
    rows = lambda n: pl.BlockSpec((1, GROUP, n), lambda i, j: (i, blocks - 1 - j, 0))
    state = pl.BlockSpec((1, 1, states, width), lambda i, j: (i, blocks - 1 - j, 0, 0))
    edge = pl.BlockSpec((1, HALO, conv_width), lambda i, j: (i, 0, 0))
    return pl.pallas_call(
        functools.partial(leave_kernel, 4),
        grid=(s, blocks),
        in_specs=[
            rows(width), rows(width), rows(width), rows(2 * states), rows(LANES), rows(LANES),
            rows(conv_width),
            pl.BlockSpec((1, 1, HALO, conv_width), lambda i, j: (i, blocks - 1 - j, 0, 0)),
            state, state, pl.BlockSpec((1, states, width), lambda i, j: (i, 0, 0)),
            rows(states), rows(states), rows(states), rows(LANES), rows(LANES),
            whole(taps.shape), whole(bias.shape), whole(step_bias.shape), whole(rate.shape),
            whole(skip.shape), whole(e.shape), whole(et.shape),
        ],
        out_specs=[rows(conv_width + LANES), edge, edge],
        out_shape=[
            jax.ShapeDtypeStruct((s, length, conv_width + LANES), BF16),
            jax.ShapeDtypeStruct((s, HALO, conv_width), F32),
            jax.ShapeDtypeStruct((s, HALO, conv_width), F32),
        ],
        scratch_shapes=[
            pltpu.VMEM((GROUP + HALO, conv_width), F32),
            pltpu.VMEM((GROUP + HALO, conv_width), F32),
            pltpu.VMEM((states, width), F32),
        ],
        compiler_params=params(),
        name="leave",
        cost_estimate=pl.CostEstimate(flops=2_000_000_000, bytes_accessed=40_000_000, transcendentals=0),
    )(
        y, x, g, bc, raw, cum, conv, before, start, fol, later, gb, gc, gc2, row, direct, taps, bias,
        step_bias, rate, skip, e, et,
    )


def chained(decay, own, axis, distance):
    leaving = own
    for _ in range(lax.axis_size(axis) - 1):
        came = shifted(leaving.astype(BF16), axis, distance)
        leaving = decay * came.astype(F32) + own
    return came


def gathered(per_slot):
    distance = 1
    while distance < lax.axis_size(CTX):
        mine = per_slot.astype(BF16)
        per_slot = mine.astype(F32) + swapped(mine, CTX, distance).astype(F32)
        distance *= 2
    mine = per_slot.astype(BF16)
    half = mine.shape[1] // 2
    first = swapped(mine, DP, 1)
    second = swapped(mine, DP, 2)
    third = swapped(first[:, :half], DP, 2)
    fourth = swapped(second[:, half:], DP, 1)
    return mine, first, second, third, fourth


def spread_kernel(counts, fill, index_ref, *refs):
    pieces = refs[:5]
    outs = refs[6:] if fill else refs[5:]
    for out in outs:
        out[...] = jnp.zeros_like(out)
    first_row = 0
    if fill:
        first_row = counts[0]
        outs[0][:, :first_row] = refs[5][...]
    slots = pieces[0].shape[0]
    half = pieces[3].shape[1]
    for source in range(4):
        for slot in range(slots):
            adapter = index_ref[source * slots + slot]
            blocks = [(0, pieces[source])] if source < 3 else [(0, pieces[3]), (half, pieces[4])]
            for start, piece in blocks:
                value = piece[slot].astype(F32)
                for row in range(0, value.shape[0], HALO):
                    number, at = divmod(start + row, counts[0])
                    at = at + (first_row if number == 0 else 0)
                    outs[number][adapter, at : at + HALO] += value[row : row + HALO]


def spread(index, pieces, counts, filled, adapters):
    width = pieces[0].shape[-1]
    rows = [count + (counts[0] if filled is not None and n == 0 else 0) for n, count in enumerate(counts)]
    more = () if filled is None else (filled,)
    return pl.pallas_call(
        functools.partial(spread_kernel, counts, filled is not None),
        in_specs=[pl.BlockSpec(memory_space=pltpu.SMEM)]
        + [pl.BlockSpec(memory_space=pltpu.VMEM)] * (5 + len(more)),
        out_specs=[pl.BlockSpec(memory_space=pltpu.VMEM)] * len(counts),
        out_shape=[jax.ShapeDtypeStruct((adapters, n, width), F32) for n in rows],
        compiler_params=params(),
        name="spread",
        cost_estimate=pl.CostEstimate(flops=1_000_000, bytes_accessed=6_000_000, transcendentals=0),
    )(index, *pieces, *more)


def partner_sum(value, kind):
    mine = value.astype(kind)
    return mine.astype(F32) + partner(mine, TENSOR).astype(F32)


def on_device(
    tokens,
    cotangent,
    lengths,
    slot_adapter_index,
    input_norm_gain,
    gate_weight_matrix,
    inner_weight_matrix,
    state_map_weight,
    step_size_weight,
    output_projection_weight,
    inner_channel_taps,
    state_map_taps,
    inner_conv_bias,
    state_map_conv_bias,
    step_size_bias,
    log_decay_rate,
    head_skip_gain,
    gated_norm_gain,
    adapter_in_down_maps,
    adapter_in_up_maps,
    adapter_out_down_maps,
    adapter_out_up_maps,
):
    slot_count, length, _ = tokens.shape
    width = gate_weight_matrix.shape[1]
    heads = step_size_bias.shape[0]
    head_dim = width // heads
    conv_width = width + state_map_weight.shape[1]
    taps_before = inner_channel_taps.shape[0] - 1
    adapter_set = adapter_in_down_maps.shape[0]
    rank = adapter_in_down_maps.shape[-1]
    spare = -heads % LANES
    rows = step_size_weight.shape[0]
    picks = jnp.broadcast_to(slot_adapter_index.astype(BF16)[None], (rows, slot_count))
    small = jnp.concatenate(
        [
            state_map_weight,
            step_size_weight,
            jnp.zeros((rows, spare - slot_count), BF16),
            picks,
        ],
        axis=1,
    )
    halo = shifted(tokens[:, length - HALO :], CTX, 1)
    inner_parts = rows_of_all(inner_weight_matrix)
    small_parts = rows_of_all(small)
    out_parts = rows_of_all(output_projection_weight)
    gate_parts = rows_of_all(gate_weight_matrix)
    all_slots = jnp.concatenate([part[0, -slot_count:] for part in small_parts[:4]])
    picked_by = all_slots.astype(jnp.int32)
    index = jnp.concatenate([slot_adapter_index, lax.axis_index(DP)[None].astype(jnp.int32)])
    places = lax.axis_index(CTX) * length + jnp.arange(length, dtype=jnp.int32)
    live_mask = (places[None, :] < lengths[:, None]).astype(F32)[..., None]
    selector = (
        slot_adapter_index[:, None] == jnp.arange(adapter_set, dtype=jnp.int32)[None, :]
    ).astype(BF16)

    head_of = jnp.arange(width, dtype=jnp.int32) // head_dim
    e = (jnp.arange(LANES, dtype=jnp.int32)[:, None] == head_of[None, :]).astype(BF16)
    et = (head_of[:, None] == jnp.arange(LANES, dtype=jnp.int32)[None, :]).astype(BF16)
    step_bias = jnp.pad(step_size_bias, (0, spare))[None]
    rate = jnp.pad(-jnp.exp(log_decay_rate), (0, spare))[None]
    skip = jnp.repeat(head_skip_gain, head_dim)[None]
    gain = gated_norm_gain[None]
    taps = jnp.concatenate([inner_channel_taps, state_map_taps], axis=1)
    conv_bias = jnp.concatenate([inner_conv_bias, state_map_conv_bias])[None]
    grad_branch = (cotangent.astype(F32) * live_mask).astype(BF16)

    def chosen(table):
        flat = table.reshape(adapter_set, -1, table.shape[-1])
        picked = jnp.einsum("sa,apq->spq", selector, flat, preferred_element_type=F32).astype(BF16)
        return picked.reshape(slot_count, *table.shape[1:])

    in_down = chosen(adapter_in_down_maps)
    in_up = chosen(adapter_in_up_maps)
    out_down = chosen(adapter_out_down_maps.transpose(0, 2, 1))
    out_up = chosen(adapter_out_up_maps)
    grad_low_out = rows_by_rows(grad_branch, out_up)

    normed, low_in, conv, x, bc, raw, cum, loc, before, packed_full = enter(
        index, tokens, halo, input_norm_gain[None], inner_parts + small_parts, adapter_in_down_maps,
        adapter_in_up_maps, taps, conv_bias, step_bias, rate, e, width, conv_width,
    )
    device_decay = jnp.exp(jnp.sum(cum[:, GROUP - 1 :: GROUP, :heads], axis=1))
    device_decay = jnp.repeat(device_decay, head_dim, axis=1)[:, None, :]
    came = chained(device_decay, loc[:, -1], CTX, 1)
    y = inside(x, bc, raw, cum, step_bias, skip)
    pair = jnp.concatenate(split(grad_low_out), axis=-1)
    twice = jnp.concatenate([out_down, out_down], axis=1)
    grad_normed, out_full = product(index, grad_branch, pair, out_parts, twice)
    gate, gate_full = product(index, normed, low_in, gate_parts, in_up[:, 0])
    mixer, sums, start = gated(y, bc, cum, loc, came, gate, grad_normed, gain, e)
    other = partner(sums, TENSOR)
    g, grad_gate, normed_out, fol, pend, grad_c2, row = turn_back(
        mixer, gate, grad_normed, sums, other, x, bc, cum, start, gain, skip, e, et
    )
    later = chained(device_decay, pend.astype(F32), CTX, -1)

    partial_low = rows_by_rows(normed_out, out_down)
    low_out = partner_sum(partial_low, F32).astype(BF16)
    half_out = lax.dot_general(normed_out, out_full, (((2,), (1,)), ((), ())), preferred_element_type=F32).astype(BF16)
    other_out = partner(half_out, TENSOR)
    up_out_grad = over_positions(low_out, grad_branch)
    down_out_grad = jnp.einsum(
        "str,stc->src", grad_low_out, normed_out.astype(F32), precision=lax.Precision.HIGH
    )
    up_gate_grad = over_positions(low_in, grad_gate)
    early = gathered(jnp.concatenate([up_out_grad, down_out_grad, up_gate_grad], axis=1))
    up_out_total, down_out_total, up_gate_total = spread(picked_by, early, (rank,) * 3, None, adapter_set)
    nt = (((2,), (1,)), ((), ()))
    gate_low = rows_by_rows(grad_gate, in_up[:, 0])
    gate_in = lax.dot_general(grad_gate, gate_full, nt, preferred_element_type=F32)
    gate_low, gate_in, later = lax.optimization_barrier((gate_low, gate_in, later))

    y_back, grad_b, grad_c, direct = inside_back(x, g, bc, raw, cum, step_bias, et)
    pack, edge, last = leave(
        y_back, x, g, bc, raw, cum, conv, before, start, fol, later, grad_b, grad_c, grad_c2, row,
        direct, taps, conv_bias, step_bias, rate, skip, e, et,
    )
    half_out, other_out, low_late, pack = lax.optimization_barrier((half_out, other_out, low_out, pack))
    partial_out = half_out.astype(F32) + other_out.astype(F32)
    branch = partial_out + rows_by_columns(low_late, out_up)
    result = (tokens.astype(F32) + live_mask * branch).astype(BF16)
    edge = shifted(edge[:, HALO - taps_before :].astype(BF16), CTX, -1).astype(F32)
    last = last + jnp.pad(edge, ((0, 0), (HALO - taps_before, 0), (0, 0)))
    pack = lax.dynamic_update_slice(pack, last.astype(BF16), (0, length - HALO, 0))
    up_wide = lax.optimization_barrier(
        jnp.pad(in_up[:, 1], ((0, 0), (0, 0), (0, pack.shape[-1] - width)))
    )
    inner_low = rows_by_rows(pack, up_wide)
    grad_low_sum = partner_sum(gate_low + inner_low, F32)
    up_inner_grad = lax.optimization_barrier(over_positions(low_in, pack))[..., :width]
    down_in_grad = jnp.einsum(
        "str,std->srd", grad_low_sum, normed.astype(F32), precision=lax.Precision.HIGH
    )
    late = gathered(jnp.concatenate([up_inner_grad, down_in_grad], axis=1))
    up_in_total, down_in_total = spread(picked_by, late, (rank, rank), up_gate_total, adapter_set)
    term = gate_in + lax.dot_general(pack, packed_full, nt, preferred_element_type=F32)
    partial_in = partner_sum(term, BF16)
    grad_normed_in = partial_in + jnp.einsum(
        "str,sdr->std", grad_low_sum, in_down, precision=lax.Precision.HIGH
    )
    tok = tokens.astype(F32)
    in_scale = lax.rsqrt(jnp.mean(tok * tok, axis=-1, keepdims=True) + EPSILON)
    weighted = grad_normed_in * input_norm_gain
    grad_tokens = (
        cotangent.astype(F32)
        + in_scale * weighted
        - tok * in_scale**3 * jnp.mean(tok * weighted, axis=-1, keepdims=True)
    )
    return (
        result,
        grad_tokens,
        down_in_total.transpose(0, 2, 1),
        up_in_total.reshape(adapter_set, 2, rank, width),
        down_out_total.transpose(0, 2, 1),
        up_out_total,
    )


def solution(mesh):
    in_specs = (
        P(DP, CTX, None),
        P(DP, CTX, None),
        P(DP),
        P(DP),
        P(),
        P(DP, TENSOR),
        P(DP, TENSOR),
        P(DP, None),
        P(DP, TENSOR),
        P(DP, TENSOR),
        P(None, TENSOR),
        P(),
        P(TENSOR),
        P(),
        P(TENSOR),
        P(TENSOR),
        P(TENSOR),
        P(TENSOR),
        P(),
        P(None, None, None, TENSOR),
        P(None, TENSOR, None),
        P(),
    )
    out_specs = (
        P(DP, CTX, None),
        P(DP, CTX, None),
        P(),
        P(None, None, None, TENSOR),
        P(None, TENSOR, None),
        P(),
    )

    return jax.shard_map(on_device, mesh=mesh, in_specs=in_specs, out_specs=out_specs, check_vma=False)
```

```python
import functools

import jax
import jax.numpy as jnp
from jax import lax
from jax.experimental import pallas as pl
from jax.experimental.pallas import tpu as pltpu
from jax.sharding import PartitionSpec as P


DP, CTX, TENSOR = "dp", "ctx", "tensor"
MIXER_WIDTH = 3072
GROUP = 256
EPSILON = 1e-05
LANES = 128
WIDE = 512
HALO = 8
TURN = 8
F32 = jnp.float32
BF16 = jnp.bfloat16
VMEM_LIMIT = 60 * 1024 * 1024


def shifted(block, axis, distance):
    devices = range(lax.axis_size(axis))
    route = [(i - distance, i) for i in devices if i - distance in devices]
    return lax.ppermute(block, axis, route)


def partner(value, axis):
    size = lax.axis_size(axis)
    return lax.ppermute(value, axis, [(i, (i + 1) % size) for i in range(size)])


def swapped(value, axis, distance):
    return lax.ppermute(value, axis, [(i, i ^ distance) for i in range(lax.axis_size(axis))])


def rows_of_all(block):
    half = block.shape[0] // 2
    first = swapped(block, DP, 1)
    second = swapped(block, DP, 2)
    third = swapped(first[:half], DP, 2)
    fourth = swapped(second[half:], DP, 1)
    return block, first, second, third, fourth


def dot(a, b):
    return jnp.dot(a, b, preferred_element_type=F32)


def dot_nt(a, b):
    return lax.dot_general(a, b, (((1,), (1,)), ((), ())), preferred_element_type=F32)


def dot_tn(a, b):
    return lax.dot_general(a, b, (((0,), (0,)), ((), ())), preferred_element_type=F32)


def batched(a, b, x, y):
    return lax.dot_general(a, b, (((x,), (y,)), ((0,), (0,))), preferred_element_type=F32)


def rows_by_rows(a, b):
    return batched(a, b, 2, 2)


def rows_by_columns(a, b):
    return batched(a, b, 2, 1)


def over_positions(a, b):
    return batched(a, b, 1, 1)


def split(value):
    high = value.astype(BF16)
    return high, (value - high.astype(F32)).astype(BF16)


def exact_dot(value, table):
    high, low = split(value)
    return dot(high, table) + dot(low, table)


def sigmoid(value):
    return lax.logistic(value)


def silu_grad(value):
    g = sigmoid(value)
    return g * (1.0 + value * (1.0 - g))


def params(**more):
    return pltpu.CompilerParams(vmem_limit_bytes=VMEM_LIMIT, **more)


ANYWHERE = pl.BlockSpec(memory_space=pl.ANY)


def assemble(place, groups, table, sem):
    rows = groups[0][0].shape[0]
    half = rows // 2
    copies = []
    column = 0
    for parts in groups:
        columns = pl.ds(column, parts[0].shape[1])
        column += parts[0].shape[1]
        for step, first, part in zip((0, 1, 2, 3, 3), (0, 0, 0, 0, half), parts):
            at = pl.ds(pl.multiple_of((place ^ step) * rows + first, half), part.shape[0])
            copies.append(pltpu.make_async_copy(part, table.at[at, columns], sem))
    for copy in copies:
        copy.start()
    for copy in copies:
        copy.wait()


def whole(shape):
    return pl.BlockSpec(shape, lambda *_: (0,) * len(shape))


def running_sum(value, backwards=False):
    rows = value.shape[0]
    i = lax.broadcasted_iota(jnp.int32, (rows, rows), 0)
    j = lax.broadcasted_iota(jnp.int32, (rows, rows), 1)
    table = jnp.where(i <= j if backwards else i >= j, 1.0, 0.0).astype(F32)
    return jnp.dot(table, value, precision=lax.Precision.HIGHEST, preferred_element_type=F32)


def conv_taps(ext_ref, taps_ref, bias_ref, lanes, tap_count):
    value = jnp.zeros((GROUP, LANES), F32) + bias_ref[:, lanes]
    for k in range(tap_count):
        start = HALO - (tap_count - 1) + k
        value = value + taps_ref[k : k + 1, lanes] * ext_ref[start : start + GROUP, lanes]
    return value


def enter_kernel(
    tap_count, index_ref, tok_ref, halo_ref, gain_ref, w0, w1, w2, w3, w4, v0, v1, v2, v3, v4,
    down_ref, up_ref, taps_ref,
    bias_ref, step_bias_ref, rate_ref, e_ref,
    normed_ref, low_ref, conv_ref, x_ref, bc_ref, raw_ref, cum_ref, loc_ref, before_ref, full_ref,
    ext, state, w_ref, sem, out_sem,
):
    b = pl.program_id(1)
    keep = pltpu.make_async_copy(w_ref, full_ref, out_sem)

    @pl.when((pl.program_id(0) == 0) & (b == 0))
    def _():
        assemble(index_ref[pl.num_programs(0)], [(w0, w1, w2, w3, w4), (v0, v1, v2, v3, v4)], w_ref, sem)
        keep.start()

    width = x_ref.shape[-1]
    conv_width = conv_ref.shape[-1]

    def project(tok, rows):
        tok = tok.astype(F32)
        scale = lax.rsqrt(jnp.mean(tok * tok, axis=-1, keepdims=True) + EPSILON)
        normed = (tok * scale * gain_ref[...]).astype(BF16)
        low = dot(normed, down_ref[0]).astype(BF16)
        for at in range(0, width, WIDE):
            columns = slice(at, at + WIDE)
            inner = dot(normed, w_ref[:, columns]) + dot(low, up_ref[0, 1, :, columns])
            ext[rows, columns] = inner.astype(BF16).astype(F32)
        rest = dot(normed, w_ref[:, width:])
        ext[rows, width:] = rest[:, : conv_width - width].astype(BF16).astype(F32)
        return normed, low, rest

    @pl.when(b == 0)
    def _():
        project(halo_ref[0], slice(0, HALO))
        state[...] = jnp.zeros_like(state)

    @pl.when(b > 0)
    def _():
        ext[:HALO] = ext[GROUP:]

    before_ref[0, 0] = ext[:HALO].astype(BF16)
    normed, low, rest = project(tok_ref[0], slice(HALO, HALO + GROUP))
    normed_ref[0] = normed
    low_ref[0] = low
    conv_ref[0] = ext[HALO:].astype(BF16)
    raw = rest[:, conv_width - width :]
    raw_ref[0] = raw
    step = jax.nn.softplus(raw + step_bias_ref[...])
    cum = running_sum(step * rate_ref[...])
    cum_ref[0] = cum
    last = cum[GROUP - 1 :]
    tail = jnp.exp(last - cum) * step

    for at in range(width, conv_width, LANES):
        lanes = slice(at, at + LANES)
        value = conv_taps(ext, taps_ref, bias_ref, lanes, tap_count)
        bc_ref[0, :, at - width : at - width + LANES] = (value * sigmoid(value)).astype(BF16)
    b_mat = bc_ref[0, :, : bc_ref.shape[-1] // 2]
    tail_high, tail_low = split(tail)
    decay_high, decay_low = split(jnp.broadcast_to(jnp.exp(last), (HALO, LANES)))
    for at in range(0, width, LANES):
        lanes = slice(at, at + LANES)
        value = conv_taps(ext, taps_ref, bias_ref, lanes, tap_count)
        x = (value * sigmoid(value)).astype(BF16)
        x_ref[0, :, lanes] = x
        table = e_ref[:, lanes]
        weighted = (x.astype(F32) * (dot(tail_high, table) + dot(tail_low, table))).astype(BF16)
        decay = (dot(decay_high, table) + dot(decay_low, table))[:1]
        new = decay * state[:, lanes] + dot_tn(b_mat, weighted)
        state[:, lanes] = new
        loc_ref[0, 0, :, lanes] = new

    @pl.when((pl.program_id(0) == pl.num_programs(0) - 1) & (b == pl.num_programs(1) - 1))
    def _():
        keep.wait()


def enter(index, tokens, halo, gain, w, down, up, taps, bias, step_bias, rate, e, width, conv_width):
    s, length, model = tokens.shape
    blocks = length // GROUP
    rank = down.shape[-1]
    states = (conv_width - width) // 2
    full_width = w[0].shape[1] + w[5].shape[1]
    rows = lambda n: pl.BlockSpec((1, GROUP, n), lambda i, j, _: (i, j, 0))
    out = lambda n, kind: jax.ShapeDtypeStruct((s, length, n), kind)
    return pl.pallas_call(
        functools.partial(enter_kernel, 4),
        grid_spec=pltpu.PrefetchScalarGridSpec(
            num_scalar_prefetch=1,
            grid=(s, blocks),
            in_specs=[
                rows(model),
                pl.BlockSpec((1, HALO, model), lambda i, j, _: (i, 0, 0)),
                whole(gain.shape),
                *[ANYWHERE] * 10,
                pl.BlockSpec((1, model, rank), lambda i, j, idx: (idx[i], 0, 0)),
                pl.BlockSpec((1, 2, rank, width), lambda i, j, idx: (idx[i], 0, 0, 0)),
                whole(taps.shape),
                whole(bias.shape),
                whole(step_bias.shape),
                whole(rate.shape),
                whole(e.shape),
            ],
            out_specs=[
                rows(model), rows(rank), rows(conv_width), rows(width), rows(2 * states),
                rows(LANES), rows(LANES),
                pl.BlockSpec((1, 1, states, width), lambda i, j, _: (i, j, 0, 0)),
                pl.BlockSpec((1, 1, HALO, conv_width), lambda i, j, _: (i, j, 0, 0)),
                ANYWHERE,
            ],
            scratch_shapes=[
                pltpu.VMEM((GROUP + HALO, conv_width), F32),
                pltpu.VMEM((states, width), F32),
                pltpu.VMEM((model, full_width), BF16),
                pltpu.SemaphoreType.DMA,
                pltpu.SemaphoreType.DMA,
            ],
        ),
        out_shape=[
            out(model, BF16), out(rank, BF16), out(conv_width, BF16), out(width, BF16),
            out(2 * states, BF16), out(LANES, F32), out(LANES, F32),
            jax.ShapeDtypeStruct((s, blocks, states, width), F32),
            jax.ShapeDtypeStruct((s, blocks, HALO, conv_width), BF16),
            jax.ShapeDtypeStruct((model, full_width), BF16),
        ],
        compiler_params=params(),
        name="enter",
        cost_estimate=pl.CostEstimate(flops=15_000_000_000, bytes_accessed=30_000_000, transcendentals=0),
    )(index, tokens, halo, gain, *w, down, up, taps, bias, step_bias, rate, e)


def inside_kernel(x_ref, bc_ref, raw_ref, cum_ref, step_bias_ref, skip_ref, y_ref, cum_t, step_t, scores):
    states = bc_ref.shape[-1] // 2
    heads_at = x_ref.shape[-1] // 64
    cum = cum_ref[0]
    step = jax.nn.softplus(raw_ref[0] + step_bias_ref[...])
    cum_t[...] = cum.T
    step_t[...] = step.T
    scores[...] = dot_nt(bc_ref[0, :, states:], bc_ref[0, :, :states])
    lane = lax.broadcasted_iota(jnp.int32, (GROUP, LANES), 1)
    causal = lax.broadcasted_iota(jnp.int32, (LANES, LANES), 0) >= lax.broadcasted_iota(
        jnp.int32, (LANES, LANES), 1
    )
    half = GROUP // 2

    @pl.loop(0, heads_at // TURN)
    def _(turn):
        rolled = pltpu.roll(cum, (LANES - TURN * turn) % LANES, 1)
        rows = pl.ds(pl.multiple_of(turn * TURN, TURN), TURN)
        cum_rows = cum_t[rows, :]
        step_rows = step_t[rows, :]
        for pair in range(TURN // 2):
            lanes = pl.ds(pl.multiple_of(turn * (TURN * 64) + pair * LANES, LANES), LANES)
            x = x_ref[0, :, lanes]
            top = skip_ref[:, lanes] * x[:half].astype(F32)
            bottom = skip_ref[:, lanes] * x[half:].astype(F32)
            for side in range(2):
                j = 2 * pair + side
                column = rolled[:, j : j + 1]
                cum_row = cum_rows[j : j + 1, :]
                step_row = step_rows[j : j + 1, :]
                own = jnp.where((lane < 64) == (side == 0), x, jnp.zeros_like(x))

                def mixing(r, c, masked):
                    diff = column[r] - cum_row[:, c]
                    if masked:
                        diff = jnp.where(causal, diff, -1e30)
                    return (scores[r, c] * jnp.exp(diff) * step_row[:, c]).astype(BF16)

                lo, hi = slice(0, half), slice(half, GROUP)
                top = top + dot(mixing(lo, lo, True), own[:half])
                bottom = bottom + dot(mixing(hi, lo, False), own[:half])
                bottom = bottom + dot(mixing(hi, hi, True), own[half:])
            y_ref[0, :half, lanes] = top
            y_ref[0, half:, lanes] = bottom


def inside(x, bc, raw, cum, step_bias, skip):
    s, length, width = x.shape
    rows = lambda n: pl.BlockSpec((1, GROUP, n), lambda i, j: (i, j, 0))
    return pl.pallas_call(
        inside_kernel,
        grid=(s, length // GROUP),
        in_specs=[
            rows(width), rows(bc.shape[-1]), rows(LANES), rows(LANES), whole(step_bias.shape),
            whole(skip.shape),
        ],
        out_specs=rows(width),
        out_shape=jax.ShapeDtypeStruct((s, length, width), F32),
        scratch_shapes=[
            pltpu.VMEM((LANES, GROUP), F32), pltpu.VMEM((LANES, GROUP), F32),
            pltpu.VMEM((GROUP, GROUP), F32),
        ],
        compiler_params=params(),
        name="inside",
        cost_estimate=pl.CostEstimate(flops=10_000_000_000, bytes_accessed=20_000_000, transcendentals=0),
    )(x, bc, raw, cum, step_bias, skip)


def product_kernel(
    index_ref, a_ref, low_ref, w0, w1, w2, w3, w4, up_ref, out_ref, full_ref, w_ref, sem, out_sem
):
    keep = pltpu.make_async_copy(w_ref, full_ref, out_sem)

    @pl.when((pl.program_id(0) == 0) & (pl.program_id(1) == 0))
    def _():
        assemble(index_ref[pl.num_programs(0)], [(w0, w1, w2, w3, w4)], w_ref, sem)
        keep.start()

    a = a_ref[0]
    low = low_ref[0]
    for at in range(0, out_ref.shape[-1], WIDE):
        columns = slice(at, at + WIDE)
        out_ref[0, :, columns] = dot(a, w_ref[:, columns]) + dot(low, up_ref[0, :, columns])

    @pl.when((pl.program_id(0) == pl.num_programs(0) - 1) & (pl.program_id(1) == pl.num_programs(1) - 1))
    def _():
        keep.wait()


def product(index, a, low, w, up):
    s, length, depth = a.shape
    width = w[0].shape[1]
    tile = min(length, 2 * GROUP)
    return pl.pallas_call(
        product_kernel,
        grid_spec=pltpu.PrefetchScalarGridSpec(
            num_scalar_prefetch=1,
            grid=(s, length // tile),
            in_specs=[
                pl.BlockSpec((1, tile, depth), lambda i, j, _: (i, j, 0)),
                pl.BlockSpec((1, tile, low.shape[-1]), lambda i, j, _: (i, j, 0)),
                *[ANYWHERE] * 5,
                pl.BlockSpec((1,) + up.shape[1:], lambda i, j, _: (i, 0, 0)),
            ],
            out_specs=[pl.BlockSpec((1, tile, width), lambda i, j, _: (i, j, 0)), ANYWHERE],
            scratch_shapes=[
                pltpu.VMEM((depth, width), BF16), pltpu.SemaphoreType.DMA, pltpu.SemaphoreType.DMA,
            ],
        ),
        out_shape=[
            jax.ShapeDtypeStruct((s, length, width), F32), jax.ShapeDtypeStruct((depth, width), BF16)
        ],
        compiler_params=params(),
        name="product",
        cost_estimate=pl.CostEstimate(
            flops=2 * s * length * depth * width, bytes_accessed=15_000_000, transcendentals=0
        ),
    )(index, a, low, *w, up)


def gated_kernel(
    y_ref, bc_ref, cum_ref, loc_ref, in_ref, gate_ref, gn_ref, gain_ref, e_ref,
    mixer_ref, sums_ref, start_ref, entering,
):
    b = pl.program_id(1)
    states = bc_ref.shape[-1] // 2
    width = y_ref.shape[-1]
    cum = cum_ref[0]
    c_mat = bc_ref[0, :, states:]
    rise_high, rise_low = split(jnp.exp(cum))
    squares = jnp.zeros((GROUP, LANES), F32)
    crosses = jnp.zeros((GROUP, LANES), F32)

    for at in range(0, width, LANES):
        lanes = slice(at, at + LANES)
        table = e_ref[:, lanes]
        rise = dot(rise_high, table) + dot(rise_low, table)

        @pl.when(b == 0)
        def _():
            entering[:, lanes] = in_ref[0, :, lanes].astype(F32)

        own = jnp.where(b == 0, 0.0, loc_ref[0, 0, :, lanes])
        start = (entering[:, lanes] + own).astype(BF16)
        start_ref[0, 0, :, lanes] = start
        entering[:, lanes] = entering[:, lanes] * rise[GROUP - 1 :]
        mixer = y_ref[0, :, lanes] + dot(c_mat, start) * rise
        mixer_ref[0, :, lanes] = mixer
        gate = gate_ref[0, :, lanes]
        gated = mixer * (gate * sigmoid(gate))
        squares = squares + gated * gated
        crosses = crosses + gated * (gn_ref[0, :, lanes] * gain_ref[:, lanes])
    lane = lax.broadcasted_iota(jnp.int32, (GROUP, LANES), 1)
    square = jnp.sum(squares, axis=-1, keepdims=True)
    cross = jnp.sum(crosses, axis=-1, keepdims=True)
    both = jnp.where(lane == 0, square, jnp.where(lane == 1, cross, 0.0))
    sums_ref[0] = both.T[:HALO]


def gated(y, bc, cum, loc, came, gate, gn, gain, e):
    s, length, width = y.shape
    blocks = length // GROUP
    states = bc.shape[-1] // 2
    rows = lambda n: pl.BlockSpec((1, GROUP, n), lambda i, j: (i, j, 0))
    return pl.pallas_call(
        gated_kernel,
        grid=(s, blocks),
        in_specs=[
            rows(width), rows(2 * states), rows(LANES),
            pl.BlockSpec((1, 1, states, width), lambda i, j: (i, jnp.maximum(j - 1, 0), 0, 0)),
            pl.BlockSpec((1, states, width), lambda i, j: (i, 0, 0)),
            rows(width), rows(width), whole(gain.shape), whole(e.shape),
        ],
        out_specs=[
            rows(width),
            pl.BlockSpec((1, HALO, GROUP), lambda i, j: (i, 0, j)),
            pl.BlockSpec((1, 1, states, width), lambda i, j: (i, j, 0, 0)),
        ],
        out_shape=[
            jax.ShapeDtypeStruct((s, length, width), F32),
            jax.ShapeDtypeStruct((s, HALO, length), F32),
            jax.ShapeDtypeStruct((s, blocks, states, width), BF16),
        ],
        scratch_shapes=[pltpu.VMEM((states, width), F32)],
        compiler_params=params(),
        name="gated",
        cost_estimate=pl.CostEstimate(flops=500_000_000, bytes_accessed=30_000_000, transcendentals=0),
    )(y, bc, cum, loc, came, gate, gn, gain, e)


def turn_kernel(
    mixer_ref, gate_ref, gn_ref, sums_ref, other_ref, x_ref, bc_ref, cum_ref, start_ref, gain_ref,
    skip_ref, e_ref, et_ref,
    g_ref, gg_ref, nout_ref, fol_ref, pend_ref, gc_ref, row_ref, pending,
):
    j = pl.program_id(1)
    states = bc_ref.shape[-1] // 2
    width = x_ref.shape[-1]
    c_mat = bc_ref[0, :, states:]
    both = (sums_ref[0] + other_ref[0]).T
    scale = lax.rsqrt(both[:, 0:1] / MIXER_WIDTH + EPSILON)
    pull = scale * scale * scale * (both[:, 1:2] / MIXER_WIDTH)
    rise_high, rise_low = split(jnp.exp(cum_ref[0]))
    grad_c = jnp.zeros((GROUP, states), F32)
    row = jnp.zeros((GROUP, LANES), F32)
    for at in range(0, width, LANES):
        lanes = slice(at, at + LANES)
        table = e_ref[:, lanes]
        rise = dot(rise_high, table) + dot(rise_low, table)
        gate = gate_ref[0, :, lanes]
        mixer = mixer_ref[0, :, lanes]
        sig = sigmoid(gate)
        silu = gate * sig
        value = mixer * silu
        gain = gain_ref[:, lanes]
        nout_ref[0, :, lanes] = (value * scale * gain).astype(BF16)
        grad = scale * (gn_ref[0, :, lanes] * gain) - value * pull
        g = (grad * silu).astype(BF16)
        g_ref[0, :, lanes] = g
        gg_ref[0, :, lanes] = (grad * mixer * (sig * (1.0 + gate * (1.0 - sig)))).astype(BF16)
        gf = g.astype(F32)
        scaled = (gf * rise).astype(BF16)
        grad_c = grad_c + dot_nt(scaled, start_ref[0, 0, :, lanes])
        own = mixer - skip_ref[:, lanes] * x_ref[0, :, lanes].astype(F32)
        row = row + exact_dot(gf * own, et_ref[lanes, :])
        before = jnp.where(j == 0, 0.0, pending[:, lanes])
        fol_ref[0, 0, :, lanes] = before
        new = dot_tn(c_mat, scaled) + rise[GROUP - 1 :] * before
        pending[:, lanes] = new
        pend_ref[0, :, lanes] = new.astype(BF16)
    gc_ref[0] = grad_c
    row_ref[0] = row


def turn_back(mixer, gate, gn, sums, other, x, bc, cum, start, gain, skip, e, et):
    s, length, width = x.shape
    blocks = length // GROUP
    states = bc.shape[-1] // 2
    rows = lambda n: pl.BlockSpec((1, GROUP, n), lambda i, j: (i, blocks - 1 - j, 0))
    state = pl.BlockSpec((1, 1, states, width), lambda i, j: (i, blocks - 1 - j, 0, 0))
    sums_spec = pl.BlockSpec((1, HALO, GROUP), lambda i, j: (i, 0, blocks - 1 - j))
    out = lambda n, kind: jax.ShapeDtypeStruct((s, length, n), kind)
    return pl.pallas_call(
        turn_kernel,
        grid=(s, blocks),
        in_specs=[
            rows(width), rows(width), rows(width), sums_spec, sums_spec, rows(width),
            rows(2 * states), rows(LANES), state, whole(gain.shape), whole(skip.shape),
            whole(e.shape), whole(et.shape),
        ],
        out_specs=[
            rows(width), rows(width), rows(width), state,
            pl.BlockSpec((1, states, width), lambda i, j: (i, 0, 0)),
            rows(states), rows(LANES),
        ],
        out_shape=[
            out(width, BF16), out(width, BF16), out(width, BF16),
            jax.ShapeDtypeStruct((s, blocks, states, width), F32),
            jax.ShapeDtypeStruct((s, states, width), BF16),
            out(states, F32), out(LANES, F32),
        ],
        scratch_shapes=[pltpu.VMEM((states, width), F32)],
        compiler_params=params(),
        name="turn_back",
        cost_estimate=pl.CostEstimate(flops=2_000_000_000, bytes_accessed=35_000_000, transcendentals=0),
    )(mixer, gate, gn, sums, other, x, bc, cum, start, gain, skip, e, et)


def inside_back_kernel(
    x_ref, g_ref, bc_ref, raw_ref, cum_ref, step_bias_ref, et_ref,
    y_ref, gb_ref, gc_ref, direct_ref, cum_t, scores, grad_scores,
):
    states = bc_ref.shape[-1] // 2
    width = x_ref.shape[-1]
    cum = cum_ref[0]
    step = jax.nn.softplus(raw_ref[0] + step_bias_ref[...])
    cum_t[...] = cum.T
    b_mat = bc_ref[0, :, :states]
    c_mat = bc_ref[0, :, states:]
    scores[...] = dot_nt(b_mat, c_mat)
    grad_scores[...] = jnp.zeros_like(grad_scores)
    lane = lax.broadcasted_iota(jnp.int32, (GROUP, LANES), 1)
    causal = lax.broadcasted_iota(jnp.int32, (LANES, LANES), 0) <= lax.broadcasted_iota(
        jnp.int32, (LANES, LANES), 1
    )
    half = GROUP // 2
    direct_ref[0] = jnp.zeros((GROUP, LANES), F32)

    @pl.loop(0, width // 64 // TURN)
    def _(turn):
        shift = (LANES - TURN * turn) % LANES
        rolled = pltpu.roll(cum, shift, 1)
        rolled_step = pltpu.roll(step, shift, 1)
        cum_rows = cum_t[pl.ds(pl.multiple_of(turn * TURN, TURN), TURN), :]
        for pair in range(TURN // 2):
            at = pl.multiple_of(turn * (TURN * 64) + pair * LANES, LANES)
            lanes = pl.ds(at, LANES)
            x = x_ref[0, :, lanes]
            g = g_ref[0, :, lanes]
            top = jnp.zeros((half, LANES), F32)
            bottom = jnp.zeros((half, LANES), F32)
            for side in range(2):
                j = 2 * pair + side
                column = rolled[:, j : j + 1]
                step_column = rolled_step[:, j : j + 1]
                row = cum_rows[j : j + 1, :]
                own = jnp.where((lane < 64) == (side == 0), g, jnp.zeros_like(g))
                lo, hi = slice(0, half), slice(half, GROUP)

                def tile(r, c, masked):
                    diff = row[:, c] - column[r]
                    if masked:
                        diff = jnp.where(causal, diff, -1e30)
                    decay = jnp.exp(diff)
                    grad_mix = dot_nt(x[r], own[c])
                    grad_scores[r, c] += grad_mix * (decay * step_column[r])
                    return dot((scores[r, c] * decay).astype(BF16), own[c])

                top = top + tile(lo, lo, True) + tile(lo, hi, False)
                bottom = bottom + tile(hi, hi, True)
            y_ref[0, :half, lanes] = top
            y_ref[0, half:, lanes] = bottom
            et = et_ref[lanes, :]
            direct_ref[0, :half] += exact_dot(top * x[:half].astype(F32), et)
            direct_ref[0, half:] += exact_dot(bottom * x[half:].astype(F32), et)

    high, low = split(grad_scores[...])
    gb_ref[0] = dot(high, c_mat) + dot(low, c_mat)
    gc_ref[0] = dot_tn(high, b_mat) + dot_tn(low, b_mat)


def inside_back(x, g, bc, raw, cum, step_bias, et):
    s, length, width = x.shape
    states = bc.shape[-1] // 2
    rows = lambda n: pl.BlockSpec((1, GROUP, n), lambda i, j: (i, j, 0))
    out = lambda n: jax.ShapeDtypeStruct((s, length, n), F32)
    return pl.pallas_call(
        inside_back_kernel,
        grid=(s, length // GROUP),
        in_specs=[
            rows(width), rows(width), rows(2 * states), rows(LANES), rows(LANES),
            whole(step_bias.shape), whole(et.shape),
        ],
        out_specs=[rows(width), rows(states), rows(states), rows(LANES)],
        out_shape=[out(width), out(states), out(states), out(LANES)],
        scratch_shapes=[
            pltpu.VMEM((LANES, GROUP), F32), pltpu.VMEM((GROUP, GROUP), F32),
            pltpu.VMEM((GROUP, GROUP), F32),
        ],
        compiler_params=params(),
        name="inside_back",
        cost_estimate=pl.CostEstimate(flops=20_000_000_000, bytes_accessed=20_000_000, transcendentals=0),
    )(x, g, bc, raw, cum, step_bias, et)


def leave_kernel(
    tap_count, y_ref, x_ref, g_ref, bc_ref, raw_ref, cum_ref, conv_ref, before_ref, start_ref, fol_ref,
    later_ref, gb_ref, gc_ref, gc2_ref, row_ref, direct_ref, taps_ref, bias_ref, step_bias_ref,
    rate_ref, skip_ref, e_ref, et_ref,
    pack_ref, edge_ref, last_ref,
    ext, back, later,
):
    j = pl.program_id(1)
    width = x_ref.shape[-1]
    conv_width = conv_ref.shape[-1]
    states = (conv_width - width) // 2
    b_mat = bc_ref[0, :, :states]
    cum = cum_ref[0]
    raw = raw_ref[0] + step_bias_ref[...]
    step = jax.nn.softplus(raw)
    last = cum[GROUP - 1 :]
    fade = jnp.exp(last - cum)
    tail = fade * step
    tail_high, tail_low = split(tail)
    step_high, step_low = split(step)
    decay_high, decay_low = split(jnp.broadcast_to(jnp.exp(last), (HALO, LANES)))
    ext[:HALO] = before_ref[0, 0].astype(F32)
    ext[HALO:] = conv_ref[0].astype(F32)

    @pl.when(j == 0)
    def _():
        back[GROUP:] = jnp.zeros((HALO, conv_width), F32)

    @pl.when(j > 0)
    def _():
        back[GROUP:] = back[:HALO]

    grad_tail = jnp.zeros((GROUP, LANES), F32)
    grad_b = gb_ref[0]
    block_decay = jnp.zeros((HALO, LANES), F32)

    def through_conv(lanes, grad):
        value = conv_taps(ext, taps_ref, bias_ref, lanes, tap_count)
        back[:GROUP, lanes] = grad * silu_grad(value)
        total = jnp.zeros((GROUP, LANES), F32)
        for k in range(tap_count):
            ahead = tap_count - 1 - k
            total = total + taps_ref[k : k + 1, lanes] * back[ahead : ahead + GROUP, lanes]
        pack_ref[0, :, lanes] = total.astype(BF16)
        last_ref[0, :, lanes] = jnp.where(j == 0, total[GROUP - HALO :], last_ref[0, :, lanes])

    for at in range(0, width, LANES):
        lanes = slice(at, at + LANES)
        table = e_ref[:, lanes]
        et = et_ref[lanes, :]

        @pl.when(j == 0)
        def _():
            later[:, lanes] = later_ref[0, :, lanes].astype(F32)

        x = x_ref[0, :, lanes].astype(F32)
        whole_grad = later[:, lanes] + fol_ref[0, 0, :, lanes]
        fresh = whole_grad.astype(BF16)
        start = start_ref[0, 0, :, lanes].astype(F32)
        decay = (dot(decay_high, table) + dot(decay_low, table))[:1]
        later[:, lanes] = later[:, lanes] * decay
        product = jnp.sum(whole_grad * start, axis=0, keepdims=True)
        block_decay = block_decay + exact_dot(jnp.broadcast_to(product, (HALO, LANES)), et)
        tails = dot(tail_high, table) + dot(tail_low, table)
        steps = dot(step_high, table) + dot(step_low, table)
        by_b = dot(b_mat, fresh)
        weighted = (x * tails).astype(BF16)
        grad_b = grad_b + dot_nt(weighted, fresh)
        grad_tail = grad_tail + exact_dot(by_b * x, et)
        grad_x = (
            steps * y_ref[0, :, lanes]
            + skip_ref[:, lanes] * g_ref[0, :, lanes].astype(F32)
            + by_b * tails
        )
        through_conv(lanes, grad_x)
    through_conv(slice(width, width + states), grad_b)
    through_conv(slice(width + states, conv_width), gc_ref[0] + gc2_ref[0])

    direct = direct_ref[0]
    tail_pull = grad_tail * tail
    end_pull = jnp.sum(tail_pull, axis=0, keepdims=True) + block_decay[:1] * jnp.exp(last)
    at_end = lax.broadcasted_iota(jnp.int32, (GROUP, LANES), 0) == GROUP - 1
    grad_cum = row_ref[0] - step * direct - tail_pull + jnp.where(at_end, end_pull, 0.0)
    grad_step = direct + grad_tail * fade + running_sum(grad_cum, True) * rate_ref[...]
    lane = lax.broadcasted_iota(jnp.int32, (GROUP, LANES), 1)
    grad_raw = jnp.where(lane < width // 64, grad_step * sigmoid(raw), 0.0)
    pack_ref[0, :, conv_width:] = grad_raw.astype(BF16)

    rows = []
    for position in range(-HALO, 0):
        total = jnp.zeros((1, conv_width), F32)
        for k in range(tap_count):
            at = position + tap_count - 1 - k
            if at >= 0:
                total = total + taps_ref[k : k + 1, :] * back[at : at + 1, :]
        rows.append(total)
    edge_ref[0] = jnp.concatenate(rows, axis=0)


def leave(
    y, x, g, bc, raw, cum, conv, before, start, fol, later, gb, gc, gc2, row, direct, taps, bias,
    step_bias, rate, skip, e, et,
):
    s, length, width = x.shape
    conv_width = conv.shape[-1]
    blocks = length // GROUP
    states = bc.shape[-1] // 2
    rows = lambda n: pl.BlockSpec((1, GROUP, n), lambda i, j: (i, blocks - 1 - j, 0))
    state = pl.BlockSpec((1, 1, states, width), lambda i, j: (i, blocks - 1 - j, 0, 0))
    edge = pl.BlockSpec((1, HALO, conv_width), lambda i, j: (i, 0, 0))
    return pl.pallas_call(
        functools.partial(leave_kernel, 4),
        grid=(s, blocks),
        in_specs=[
            rows(width), rows(width), rows(width), rows(2 * states), rows(LANES), rows(LANES),
            rows(conv_width),
            pl.BlockSpec((1, 1, HALO, conv_width), lambda i, j: (i, blocks - 1 - j, 0, 0)),
            state, state, pl.BlockSpec((1, states, width), lambda i, j: (i, 0, 0)),
            rows(states), rows(states), rows(states), rows(LANES), rows(LANES),
            whole(taps.shape), whole(bias.shape), whole(step_bias.shape), whole(rate.shape),
            whole(skip.shape), whole(e.shape), whole(et.shape),
        ],
        out_specs=[rows(conv_width + LANES), edge, edge],
        out_shape=[
            jax.ShapeDtypeStruct((s, length, conv_width + LANES), BF16),
            jax.ShapeDtypeStruct((s, HALO, conv_width), F32),
            jax.ShapeDtypeStruct((s, HALO, conv_width), F32),
        ],
        scratch_shapes=[
            pltpu.VMEM((GROUP + HALO, conv_width), F32),
            pltpu.VMEM((GROUP + HALO, conv_width), F32),
            pltpu.VMEM((states, width), F32),
        ],
        compiler_params=params(),
        name="leave",
        cost_estimate=pl.CostEstimate(flops=2_000_000_000, bytes_accessed=40_000_000, transcendentals=0),
    )(
        y, x, g, bc, raw, cum, conv, before, start, fol, later, gb, gc, gc2, row, direct, taps, bias,
        step_bias, rate, skip, e, et,
    )


def chained(decay, own, axis, distance):
    leaving = own
    for _ in range(lax.axis_size(axis) - 1):
        came = shifted(leaving.astype(BF16), axis, distance)
        leaving = decay * came.astype(F32) + own
    return came


def gathered(per_slot):
    distance = 1
    while distance < lax.axis_size(CTX):
        mine = per_slot.astype(BF16)
        per_slot = mine.astype(F32) + swapped(mine, CTX, distance).astype(F32)
        distance *= 2
    mine = per_slot.astype(BF16)
    half = mine.shape[1] // 2
    first = swapped(mine, DP, 1)
    second = swapped(mine, DP, 2)
    third = swapped(first[:, :half], DP, 2)
    fourth = swapped(second[:, half:], DP, 1)
    return mine, first, second, third, fourth


def spread_kernel(counts, fill, index_ref, *refs):
    pieces = refs[:5]
    outs = refs[6:] if fill else refs[5:]
    for out in outs:
        out[...] = jnp.zeros_like(out)
    first_row = 0
    if fill:
        first_row = counts[0]
        outs[0][:, :first_row] = refs[5][...]
    slots = pieces[0].shape[0]
    half = pieces[3].shape[1]
    for source in range(4):
        for slot in range(slots):
            adapter = index_ref[source * slots + slot]
            blocks = [(0, pieces[source])] if source < 3 else [(0, pieces[3]), (half, pieces[4])]
            for start, piece in blocks:
                value = piece[slot].astype(F32)
                for row in range(0, value.shape[0], HALO):
                    number, at = divmod(start + row, counts[0])
                    at = at + (first_row if number == 0 else 0)
                    outs[number][adapter, at : at + HALO] += value[row : row + HALO]


def spread(index, pieces, counts, filled, adapters):
    width = pieces[0].shape[-1]
    rows = [count + (counts[0] if filled is not None and n == 0 else 0) for n, count in enumerate(counts)]
    more = () if filled is None else (filled,)
    return pl.pallas_call(
        functools.partial(spread_kernel, counts, filled is not None),
        in_specs=[pl.BlockSpec(memory_space=pltpu.SMEM)]
        + [pl.BlockSpec(memory_space=pltpu.VMEM)] * (5 + len(more)),
        out_specs=[pl.BlockSpec(memory_space=pltpu.VMEM)] * len(counts),
        out_shape=[jax.ShapeDtypeStruct((adapters, n, width), F32) for n in rows],
        compiler_params=params(),
        name="spread",
        cost_estimate=pl.CostEstimate(flops=1_000_000, bytes_accessed=6_000_000, transcendentals=0),
    )(index, *pieces, *more)


def partner_sum(value, kind):
    mine = value.astype(kind)
    return mine.astype(F32) + partner(mine, TENSOR).astype(F32)


def on_device(
    tokens,
    cotangent,
    lengths,
    slot_adapter_index,
    input_norm_gain,
    gate_weight_matrix,
    inner_weight_matrix,
    state_map_weight,
    step_size_weight,
    output_projection_weight,
    inner_channel_taps,
    state_map_taps,
    inner_conv_bias,
    state_map_conv_bias,
    step_size_bias,
    log_decay_rate,
    head_skip_gain,
    gated_norm_gain,
    adapter_in_down_maps,
    adapter_in_up_maps,
    adapter_out_down_maps,
    adapter_out_up_maps,
):
    slot_count, length, _ = tokens.shape
    width = gate_weight_matrix.shape[1]
    heads = step_size_bias.shape[0]
    head_dim = width // heads
    conv_width = width + state_map_weight.shape[1]
    taps_before = inner_channel_taps.shape[0] - 1
    adapter_set = adapter_in_down_maps.shape[0]
    rank = adapter_in_down_maps.shape[-1]
    spare = -heads % LANES
    rows = step_size_weight.shape[0]
    picks = jnp.broadcast_to(slot_adapter_index.astype(BF16)[None], (rows, slot_count))
    small = jnp.concatenate(
        [
            state_map_weight,
            step_size_weight,
            jnp.zeros((rows, spare - slot_count), BF16),
            picks,
        ],
        axis=1,
    )
    halo = shifted(tokens[:, length - HALO :], CTX, 1)
    inner_parts = rows_of_all(inner_weight_matrix)
    small_parts = rows_of_all(small)
    out_parts = rows_of_all(output_projection_weight)
    gate_parts = rows_of_all(gate_weight_matrix)
    all_slots = jnp.concatenate([part[0, -slot_count:] for part in small_parts[:4]])
    picked_by = all_slots.astype(jnp.int32)
    index = jnp.concatenate([slot_adapter_index, lax.axis_index(DP)[None].astype(jnp.int32)])
    places = lax.axis_index(CTX) * length + jnp.arange(length, dtype=jnp.int32)
    live_mask = (places[None, :] < lengths[:, None]).astype(F32)[..., None]
    selector = (
        slot_adapter_index[:, None] == jnp.arange(adapter_set, dtype=jnp.int32)[None, :]
    ).astype(BF16)

    head_of = jnp.arange(width, dtype=jnp.int32) // head_dim
    e = (jnp.arange(LANES, dtype=jnp.int32)[:, None] == head_of[None, :]).astype(BF16)
    et = (head_of[:, None] == jnp.arange(LANES, dtype=jnp.int32)[None, :]).astype(BF16)
    step_bias = jnp.pad(step_size_bias, (0, spare))[None]
    rate = jnp.pad(-jnp.exp(log_decay_rate), (0, spare))[None]
    skip = jnp.repeat(head_skip_gain, head_dim)[None]
    gain = gated_norm_gain[None]
    taps = jnp.concatenate([inner_channel_taps, state_map_taps], axis=1)
    conv_bias = jnp.concatenate([inner_conv_bias, state_map_conv_bias])[None]
    grad_branch = (cotangent.astype(F32) * live_mask).astype(BF16)

    def chosen(table):
        flat = table.reshape(adapter_set, -1, table.shape[-1])
        picked = jnp.einsum("sa,apq->spq", selector, flat, preferred_element_type=F32).astype(BF16)
        return picked.reshape(slot_count, *table.shape[1:])

    in_down = chosen(adapter_in_down_maps)
    in_up = chosen(adapter_in_up_maps)
    out_down = chosen(adapter_out_down_maps.transpose(0, 2, 1))
    out_up = chosen(adapter_out_up_maps)
    grad_low_out = rows_by_rows(grad_branch, out_up)

    normed, low_in, conv, x, bc, raw, cum, loc, before, packed_full = enter(
        index, tokens, halo, input_norm_gain[None], inner_parts + small_parts, adapter_in_down_maps,
        adapter_in_up_maps, taps, conv_bias, step_bias, rate, e, width, conv_width,
    )
    device_decay = jnp.exp(jnp.sum(cum[:, GROUP - 1 :: GROUP, :heads], axis=1))
    device_decay = jnp.repeat(device_decay, head_dim, axis=1)[:, None, :]
    came = chained(device_decay, loc[:, -1], CTX, 1)
    y = inside(x, bc, raw, cum, step_bias, skip)
    pair = jnp.concatenate(split(grad_low_out), axis=-1)
    twice = jnp.concatenate([out_down, out_down], axis=1)
    grad_normed, out_full = product(index, grad_branch, pair, out_parts, twice)
    gate, gate_full = product(index, normed, low_in, gate_parts, in_up[:, 0])
    mixer, sums, start = gated(y, bc, cum, loc, came, gate, grad_normed, gain, e)
    other = partner(sums, TENSOR)
    g, grad_gate, normed_out, fol, pend, grad_c2, row = turn_back(
        mixer, gate, grad_normed, sums, other, x, bc, cum, start, gain, skip, e, et
    )
    later = chained(device_decay, pend.astype(F32), CTX, -1)

    partial_low = rows_by_rows(normed_out, out_down)
    low_out = partner_sum(partial_low, F32).astype(BF16)
    half_out = lax.dot_general(normed_out, out_full, (((2,), (1,)), ((), ())), preferred_element_type=F32).astype(BF16)
    other_out = partner(half_out, TENSOR)
    up_out_grad = over_positions(low_out, grad_branch)
    down_out_grad = jnp.einsum(
        "str,stc->src", grad_low_out, normed_out.astype(F32), precision=lax.Precision.HIGH
    )
    up_gate_grad = over_positions(low_in, grad_gate)
    early = gathered(jnp.concatenate([up_out_grad, down_out_grad, up_gate_grad], axis=1))
    up_out_total, down_out_total, up_gate_total = spread(picked_by, early, (rank,) * 3, None, adapter_set)
    nt = (((1,), (1,)), ((), ()))
    gate_low = rows_by_rows(grad_gate, in_up[:, 0])
    gate_in = [
        lax.dot_general(grad_gate[s], gate_full, nt, preferred_element_type=F32)
        for s in range(slot_count)
    ]
    gate_low, gate_in, later = lax.optimization_barrier((gate_low, gate_in, later))

    y_back, grad_b, grad_c, direct = inside_back(x, g, bc, raw, cum, step_bias, et)
    pack, edge, last = leave(
        y_back, x, g, bc, raw, cum, conv, before, start, fol, later, grad_b, grad_c, grad_c2, row,
        direct, taps, conv_bias, step_bias, rate, skip, e, et,
    )
    half_out, other_out, low_late, pack = lax.optimization_barrier((half_out, other_out, low_out, pack))
    partial_out = half_out.astype(F32) + other_out.astype(F32)
    branch = partial_out + rows_by_columns(low_late, out_up)
    result = (tokens.astype(F32) + live_mask * branch).astype(BF16)
    edge = shifted(edge[:, HALO - taps_before :].astype(BF16), CTX, -1).astype(F32)
    last = last + jnp.pad(edge, ((0, 0), (HALO - taps_before, 0), (0, 0)))
    pack = lax.dynamic_update_slice(pack, last.astype(BF16), (0, length - HALO, 0))
    up_wide = lax.optimization_barrier(
        jnp.pad(in_up[:, 1], ((0, 0), (0, 0), (0, pack.shape[-1] - width)))
    )
    inner_low = rows_by_rows(pack, up_wide)
    grad_low_sum = partner_sum(gate_low + inner_low, F32)
    up_inner_grad = lax.optimization_barrier(over_positions(low_in, pack))[..., :width]
    down_in_grad = jnp.einsum(
        "str,std->srd", grad_low_sum, normed.astype(F32), precision=lax.Precision.HIGH
    )
    late = gathered(jnp.concatenate([up_inner_grad, down_in_grad], axis=1))
    up_in_total, down_in_total = spread(picked_by, late, (rank, rank), up_gate_total, adapter_set)
    terms = []
    for s in range(slot_count):
        term = gate_in[s] + lax.dot_general(pack[s], packed_full, nt, preferred_element_type=F32)
        terms.append(partner_sum(term, BF16))
    partial_in = jnp.stack(terms)
    grad_normed_in = partial_in + jnp.einsum(
        "str,sdr->std", grad_low_sum, in_down, precision=lax.Precision.HIGH
    )
    tok = tokens.astype(F32)
    in_scale = lax.rsqrt(jnp.mean(tok * tok, axis=-1, keepdims=True) + EPSILON)
    weighted = grad_normed_in * input_norm_gain
    grad_tokens = (
        cotangent.astype(F32)
        + in_scale * weighted
        - tok * in_scale**3 * jnp.mean(tok * weighted, axis=-1, keepdims=True)
    )
    return (
        result,
        grad_tokens,
        down_in_total.transpose(0, 2, 1),
        up_in_total.reshape(adapter_set, 2, rank, width),
        down_out_total.transpose(0, 2, 1),
        up_out_total,
    )


def solution(mesh):
    in_specs = (
        P(DP, CTX, None),
        P(DP, CTX, None),
        P(DP),
        P(DP),
        P(),
        P(DP, TENSOR),
        P(DP, TENSOR),
        P(DP, None),
        P(DP, TENSOR),
        P(DP, TENSOR),
        P(None, TENSOR),
        P(),
        P(TENSOR),
        P(),
        P(TENSOR),
        P(TENSOR),
        P(TENSOR),
        P(TENSOR),
        P(),
        P(None, None, None, TENSOR),
        P(None, TENSOR, None),
        P(),
    )
    out_specs = (
        P(DP, CTX, None),
        P(DP, CTX, None),
        P(),
        P(None, None, None, TENSOR),
        P(None, TENSOR, None),
        P(),
    )

    return jax.shard_map(on_device, mesh=mesh, in_specs=in_specs, out_specs=out_specs, check_vma=False)
```
